32 devices in a mesh: face: 2 (over y), ty: 4 (over x, core), tx: 4 (over z).
Axes of the slice: x: 2, y: 2, z: 4, core: 2. Of those that a mesh axis runs over, the one named last changes fastest.
Arguments:
- cotangent: float32 [2, 32, 32, 128], P('face', 'ty', 'tx'), may hold values from -6 to 6
- courant_x: float32 [2, 32, 36, 32], P('face', 'ty', 'tx'), may hold values from -0.6 to 0.6
- edge_x: float32 [2, 32, 36], P('face', 'ty', 'tx'), may hold values from 0.7 to 1.4
- courant_y: float32 [2, 36, 32, 32], P('face', 'ty', 'tx'), may hold values from -0.6 to 0.6
- edge_y: float32 [2, 36, 32], P('face', 'ty', 'tx'), may hold values from 0.7 to 1.4
- cell_area: float32 [2, 32, 32], P('face', 'ty', 'tx'), may hold values from 0.7 to 1.4
- seam_partner: int32 [2, 4], replicated, may hold values from 0 to 7, as said below
- seam_flip: int32 [2, 4], replicated, may hold values from 0 to 1, as said below
Outputs:
- sensitivity: float32 [2, 32, 32, 128], P('face', 'ty', 'tx')
The draws below stay inside these ranges and needn't reach their ends.
Inputs may be any that keep to these rules, and one draw needn't show every extreme that they name: `seam_partner`: the gluing pairs face edges: the partner of an edge's partner is that edge, and no edge is glued to itself; some east or west edge is glued to a north or south edge. `seam_flip`: the same for both edges of a glued pair.
All inputs are finite; a program needn't handle non-finite values.
Results may differ from the reference program's by a relative error of at most 0.0003.
Values sent between devices are 32-bit elements; how exact they have to be, the bound alone decides.
No kernel may reach another device: no remote copies, remote signals or barrier semaphores. Data moves between devices by JAX's collectives and lax.ppermute only.
A program may use at most 64 MiB of HBM per device.

```python
import math
import jax
import jax.numpy as jnp
from jax import lax

CX = 8
LEV = 32
NTR = 4
HALO = 3
STEPS = 2
FACES = 2
S = 32
CY = 8
LANES = 128
XIF = 36
YIF = 36
N_TY = 4
N_TX = 4


def seam_pairs(key):
    edge_count = 4 * FACES
    shuffled = jax.random.permutation(jax.random.fold_in(key, 71), edge_count).astype(jnp.int32)
    position = jnp.zeros((edge_count,), jnp.int32).at[shuffled].set(jnp.arange(edge_count, dtype=jnp.int32))
    edge_ids = jnp.arange(edge_count, dtype=jnp.int32)
    parity = edge_ids % 2
    first_x = jnp.argmin(position + edge_count * parity).astype(jnp.int32)
    first_y = jnp.argmin(position + edge_count * (1 - parity)).astype(jnp.int32)
    ranking = position.at[first_x].set(-2).at[first_y].set(-1)
    edge_order = jnp.argsort(ranking, stable=True).astype(jnp.int32)
    firsts = edge_order[0::2]
    seconds = edge_order[1::2]
    partner = jnp.zeros((edge_count,), jnp.int32).at[firsts].set(seconds).at[seconds].set(firsts)
    flip_bits = jax.random.randint(jax.random.fold_in(key, 72), (edge_count // 2,), 0, 2).astype(jnp.int32)
    flip_bits = flip_bits.at[0].set(0).at[1].set(1)
    flip_codes = jnp.zeros((edge_count,), jnp.int32).at[firsts].set(flip_bits).at[seconds].set(flip_bits)
    return (partner.reshape(FACES, 4), flip_codes.reshape(FACES, 4))


def draw_seam_partner(key, part):
    return seam_pairs(key)[0]


def draw_seam_flip(key, part):
    return seam_pairs(key)[1]


def block_levels(key, shape, pieces, smallest, top_value):
    factor_of, own = 1.0, jax.random.fold_in(key, 6)
    for dim, shards_of in pieces:
        draws = jnp.exp(jax.random.uniform(jax.random.fold_in(own, dim), (shards_of,), jnp.float32, smallest / len(pieces), top_value / len(pieces)))
        factor_of = factor_of * jnp.repeat(draws, shape[dim] // shards_of).reshape([-1 if axis == dim else 1 for axis in range(len(shape))])
    return factor_of


def bell_draw(stream_key, dims, width, most, shards=(), kind=jnp.bfloat16):
    gain = block_levels(stream_key, dims, shards, -0.22, 0.18) if shards else 1.0
    result = jax.random.normal(stream_key, dims, jnp.float32) * width * gain
    return jnp.minimum(jnp.maximum(result, -most), most).astype(kind)


def setup_inputs(seed: int = 0) -> dict:
    arg_keys = jax.random.split(jax.random.key(seed), 9)
    return {
        "cotangent": bell_draw(arg_keys[0], (FACES, S, S, LANES), 1.0, 6.0, ((0, 2), (1, 4), (2, 4)), jnp.float32),
        "courant_x": jnp.clip(jax.random.uniform(arg_keys[1], (FACES, S, XIF, LEV), jnp.float32, -0.6, 0.6) * block_levels(arg_keys[1], (FACES, S, XIF, LEV), ((0, 2), (1, 4), (2, 4)), -0.4, 0.0), -0.6, 0.6),
        "edge_x": jnp.clip(jnp.exp(math.log(1.4) - 0.6931472 * jax.random.uniform(arg_keys[2], (FACES, S, XIF), jnp.float32) ** block_levels(arg_keys[2], (FACES, S, XIF), ((0, 2), (1, 4), (2, 4)), -0.2, 0.2)), 0.7, 1.4),
        "courant_y": jnp.clip(jax.random.uniform(arg_keys[3], (FACES, YIF, S, LEV), jnp.float32, -0.6, 0.6) * block_levels(arg_keys[3], (FACES, YIF, S, LEV), ((0, 2), (1, 4), (2, 4)), -0.4, 0.0), -0.6, 0.6),
        "edge_y": jnp.clip(jnp.exp(math.log(1.4) - 0.6931472 * jax.random.uniform(arg_keys[4], (FACES, YIF, S), jnp.float32) ** block_levels(arg_keys[4], (FACES, YIF, S), ((0, 2), (1, 4), (2, 4)), -0.2, 0.2)), 0.7, 1.4),
        "cell_area": jnp.clip(jnp.exp(math.log(1.4) - 0.6931472 * jax.random.uniform(arg_keys[5], (FACES, S, S), jnp.float32) ** block_levels(arg_keys[5], (FACES, S, S), ((0, 2), (1, 4), (2, 4)), -0.2, 0.2)), 0.7, 1.4),
        "seam_partner": draw_seam_partner(jax.random.fold_in(arg_keys[8], 71), 0),
        "seam_flip": draw_seam_flip(jax.random.fold_in(arg_keys[8], 71), 0),
    }


def take_slab(source, axis_at, anchor, finish):
    return lax.slice_in_dim(source, anchor, finish, axis=axis_at)

def parabolic_sweep(extended, courant, edge_length, area_cells, axis_at):
    inner_count = extended.shape[axis_at] - 6
    interface_value = 7.0 / 12.0 * (take_slab(extended, axis_at, 1, inner_count + 4) + take_slab(extended, axis_at, 2, inner_count + 5)) - 1.0 / 12.0 * (take_slab(extended, axis_at, 0, inner_count + 3) + take_slab(extended, axis_at, 3, inner_count + 6))
    a_low = take_slab(interface_value, axis_at, 0, inner_count + 1)
    a_mid = take_slab(interface_value, axis_at, 1, inner_count + 2)
    a_high = take_slab(interface_value, axis_at, 2, inner_count + 3)
    left_cell = take_slab(extended, axis_at, 2, inner_count + 3)
    right_cell = take_slab(extended, axis_at, 3, inner_count + 4)
    curve_left = 6.0 * left_cell - 3.0 * (a_low + a_mid)
    curve_right = 6.0 * right_cell - 3.0 * (a_mid + a_high)
    upwind = -courant
    from_left = a_mid - 0.5 * courant * (a_mid - a_low - (1.0 - courant * (2.0 / 3.0)) * curve_left)
    from_right = a_mid + 0.5 * upwind * (a_high - a_mid + (1.0 - upwind * (2.0 / 3.0)) * curve_right)
    face_value = jnp.where(courant > 0, from_left, from_right)
    flux_term = courant * edge_length * face_value
    return take_slab(extended, axis_at, 3, inner_count + 3) - (take_slab(flux_term, axis_at, 1, inner_count + 1) - take_slab(flux_term, axis_at, 0, inner_count)) / area_cells

def face_rims(field):
    east_rim = jnp.swapaxes(field[:, :, ::-1][:, :, :HALO], 1, 2)
    north_rim = field[:, ::-1][:, :HALO]
    west_rim = jnp.swapaxes(field[:, :, :HALO], 1, 2)
    south_rim = field[:, :HALO]
    return jnp.stack([east_rim, north_rim, west_rim, south_rim], axis=1)

def partner_rim(all_rims, seam_partner, seam_flip, border):
    flat_rims = all_rims.reshape((FACES * 4,) + all_rims.shape[2:])
    chosen = jnp.take(flat_rims, seam_partner[:, border], axis=0)
    flipped = chosen[:, :, ::-1]
    return jnp.where((seam_flip[:, border] == 1)[:, None, None, None], flipped, chosen)

def step_x(field, courant_x, edge_x, cell_area, seam_partner, seam_flip):
    all_rims = face_rims(field)
    east_cols = jnp.swapaxes(partner_rim(all_rims, seam_partner, seam_flip, 0), 1, 2)
    west_cols = jnp.swapaxes(partner_rim(all_rims, seam_partner, seam_flip, 2), 1, 2)[:, :, ::-1]
    extended = jnp.concatenate([west_cols, field, east_cols], axis=2)
    windows = jnp.stack([extended[:, :, column_tile * CX:column_tile * CX + CX + 6] for column_tile in range(N_TX)], axis=2)
    courant = jnp.tile(courant_x.reshape(FACES, S, N_TX, CX + 1, LEV), NTR)
    lengths = edge_x.reshape(FACES, S, N_TX, CX + 1)[..., None]
    areas = cell_area.reshape(FACES, S, N_TX, CX)[..., None]
    moved = parabolic_sweep(windows, courant, lengths, areas, 3)
    return moved.reshape(FACES, S, S, LANES)

def step_y(field, courant_y, edge_y, cell_area, seam_partner, seam_flip):
    all_rims = face_rims(field)
    north_rows = partner_rim(all_rims, seam_partner, seam_flip, 1)
    south_rows = partner_rim(all_rims, seam_partner, seam_flip, 3)[:, ::-1]
    extended = jnp.concatenate([south_rows, field, north_rows], axis=1)
    windows = jnp.stack([extended[:, row_tile * CY:row_tile * CY + CY + 6] for row_tile in range(N_TY)], axis=1)
    courant = jnp.tile(courant_y.reshape(FACES, N_TY, CY + 1, S, LEV), NTR)
    lengths = edge_y.reshape(FACES, N_TY, CY + 1, S)[..., None]
    areas = cell_area.reshape(FACES, N_TY, CY, S)[..., None]
    moved = parabolic_sweep(windows, courant, lengths, areas, 2)
    return moved.reshape(FACES, S, S, LANES)

def reference(cotangent, courant_x, edge_x, courant_y, edge_y, cell_area, seam_partner, seam_flip):

    def forward(field):
        for repeat in range(STEPS):
            field = step_x(field, courant_x, edge_x, cell_area, seam_partner, seam_flip)
            field = step_y(field, courant_y, edge_y, cell_area, seam_partner, seam_flip)
        return field
    unused, pullback = jax.vjp(forward, jnp.zeros_like(cotangent))
    return pullback(cotangent)[0]
```

```python
import functools

import jax
import jax.numpy as jnp
from jax import lax
from jax.experimental import pallas as pl
from jax.experimental.pallas import tpu as pltpu
from jax.sharding import PartitionSpec as P

STEPS = 2
AXES = ("face", "ty", "tx")
PARTS = 4
PAD = 16
VMEM = pl.BlockSpec(memory_space=pltpu.VMEM)
SMEM = pl.BlockSpec(memory_space=pltpu.SMEM)


def loop(count, body):
    if count <= 8:
        for i in range(count):
            body(i)
    else:
        lax.fori_loop(0, count, lambda i, carry: (body(i), carry)[1], 0)


def split_parts(block, width, axis):
    return [lax.slice_in_dim(block, q * width, (q + 1) * width, axis=axis) for q in range(PARTS)]


def turned(block, rows):
    return jnp.concatenate(split_parts(block.T, rows, 0), axis=1)


def pack_kernel(cot_ref, qx_ref, qy_ref, send_ref):
    cy, cx, lanes = cot_ref.shape
    levels = lanes // PARTS
    width = 3 * cx * PARTS

    def body(y):
        rows = jnp.concatenate([cot_ref[y], qx_ref[y], qy_ref[y]], axis=0)
        send_ref[:, y, 0:width] = turned(rows, levels)

    loop(cy, body)


def unpack_kernel(recv_ref, out_ref):
    cy, cx, _ = out_ref.shape

    def body(y):
        out_ref[y] = turned(recv_ref[:, y, :], cx)

    loop(cy, body)


def stencil(coefs, side):
    c_low, f_low, c_high, f_high = (
        jnp.concatenate([part] * PARTS, axis=1) for part in split_parts(coefs, side, 1)
    )

    def interface(c, f):
        size = jnp.abs(c)
        half = 0.5 * size
        w = 3.0 * half * (1.0 - (2.0 / 3.0) * size)
        plus = c > 0
        centre = f * (1.0 - half - w)
        outer = f * (half - w)
        cell = f * (2.0 * w)
        zero = jnp.zeros_like(c)
        o_low, o_high = jnp.where(plus, outer, zero), jnp.where(plus, zero, outer)
        s_low, s_high = jnp.where(plus, cell, zero), jnp.where(plus, zero, cell)
        near, far = 7.0 / 12.0, 1.0 / 12.0
        return (
            -far * o_low,
            near * o_low - far * centre,
            near * (centre + o_low) - far * o_high + s_low,
            near * (centre + o_high) - far * o_low + s_high,
            near * o_high - far * centre,
            -far * o_high,
        )

    low, high = interface(c_low, f_low), interface(c_high, f_high)
    return (
        low[0],
        low[1] - high[0],
        low[2] - high[1],
        1.0 + low[3] - high[2],
        low[4] - high[3],
        low[5] - high[4],
        -high[5],
    )


def sphere_kernel(
    tiles_high, tiles_wide, partner_ref, flip_ref, recv_ref, out_ref, beta, acc, field, prod, rim, turned_rim
):
    faces, side, lanes = field.shape
    cy, cx = side // tiles_high, side // tiles_wide
    slots = prod.shape[0]

    def assemble(i):
        f, ty = i // tiles_high, i % tiles_high
        rows = slice(ty * cy, (ty + 1) * cy) if isinstance(i, int) else pl.ds(ty * cy, cy)
        tiles = [recv_ref[i * tiles_wide + tx] for tx in range(tiles_wide)]
        for j, target in enumerate((field.at[f], acc.at[0, f], acc.at[1, f])):
            target[rows, :] = jnp.concatenate(
                [
                    tile[:, (q * 3 + j) * cx : (q * 3 + j + 1) * cx]
                    for q in range(PARTS)
                    for tile in tiles
                ],
                axis=1,
            )

    loop(faces * tiles_high, assemble)

    def coefficients(f):
        for k, value in enumerate(stencil(turned(acc[0, f], side), side)):
            beta[0, k, f] = value
        for k, value in enumerate(stencil(acc[1, f], side)):
            beta[1, k, f] = value

    loop(faces, coefficients)
    prod[...] = jnp.zeros_like(prod)
    row_id = lax.broadcasted_iota(jnp.int32, (lanes, lanes), 0)
    column_id = lax.broadcasted_iota(jnp.int32, (lanes, lanes), 1)
    mirror = jnp.zeros((lanes, lanes), jnp.float32)
    for q in range(PARTS):
        inside = (row_id >= q * side) & (row_id < (q + 1) * side)
        mirror = jnp.where(inside & (row_id + column_id == (2 * q + 1) * side - 1), 1.0, mirror)

    def sweep(d):
        def apply(f):
            cells = field[f]
            here = prod.at[f % slots]
            total = None
            for k in range(7):
                here[k, PAD : PAD + side, :] = beta[d, k, f] * cells
            for k in range(7):
                start = PAD - 8 - (k - 3)
                term = here[k, start : start + side + 16, :]
                total = term if total is None else total + term
            acc[d, f] = total[8 : 8 + side]
            acc[1 - d, f] = jnp.zeros((side, lanes), jnp.float32)
            rim[f, 0:8, :] = total[side + 8 :]
            rim[f, 8:16, :] = total[0:8]

        loop(faces, apply)
        flat = rim[...].reshape(faces * 16, lanes)
        turned_rim[...] = jnp.dot(
            flat, mirror, precision=lax.Precision.HIGHEST, preferred_element_type=jnp.float32
        ).reshape(faces, 16, lanes)
        for f in range(faces):
            for low in range(2):
                edge = 4 * f + d + 2 * low
                code = partner_ref[edge]
                flipped = flip_ref[edge] == 1
                other = code // 4
                border = code % 4
                layout = border % 2
                for depth in range(3):
                    source = 15 - depth if low else depth
                    row = jnp.where(
                        flipped,
                        turned_rim[f, source : source + 1, :],
                        rim[f, source : source + 1, :],
                    )
                    target = pl.ds(jnp.where(border < 2, side - 1 - depth, depth), 1)
                    acc[layout, other, target, :] = acc[layout, other, target, :] + row

        def merge(f):
            field[f] = turned(acc[d, f], side) + acc[1 - d, f]

        loop(faces, merge)

    for step in range(STEPS):
        sweep(1)
        sweep(0)

    def hand_out(i):
        f, ty = i // tiles_high, i % tiles_high
        rows = slice(ty * cy, (ty + 1) * cy) if isinstance(i, int) else pl.ds(ty * cy, cy)
        block = field[f, rows, :]
        for tx in range(tiles_wide):
            out_ref[i * tiles_wide + tx] = jnp.concatenate(
                [part[:, tx * cx : (tx + 1) * cx] for part in split_parts(block, side, 1)], axis=1
            )

    loop(faces * tiles_high, hand_out)


def ratios(courant, length, area, axis):
    count = courant.shape[axis]
    out = []
    for start in (0, 1):
        c = lax.slice_in_dim(courant, start, start + count - 1, axis=axis)
        e = lax.slice_in_dim(length, start, start + count - 1, axis=axis)
        out += [c, c * (e / area)[:, :, None]]
    return jnp.concatenate(out, axis=-1)


def on_device(cotangent, courant_x, edge_x, courant_y, edge_y, cell_area, seam_partner, seam_flip):
    cells = cotangent[0]
    cy, cx, lanes = cells.shape
    levels = courant_x.shape[-1]
    faces, tiles_high, tiles_wide = (lax.axis_size(axis) for axis in AXES)
    devices = faces * tiles_high * tiles_wide
    side = cx * tiles_wide
    width = PARTS * side
    if lanes != PARTS * levels or devices % levels or side != cy * tiles_high:
        raise ValueError("unsupported sizes")
    f32 = jnp.float32

    send = pl.pallas_call(
        pack_kernel,
        out_shape=jax.ShapeDtypeStruct((levels, cy, -(-3 * PARTS * cx // 128) * 128), f32),
        in_specs=[VMEM] * 3,
        out_specs=VMEM,
        name="pack",
    )(
        cells,
        ratios(courant_x[0], edge_x[0], cell_area[0], 1),
        ratios(courant_y[0], edge_y[0], cell_area[0], 0),
    )
    if devices > levels:
        send = jnp.tile(send, (devices // levels, 1, 1))
    spheres = lax.all_to_all(send, AXES, 0, 0, tiled=True)
    result = pl.pallas_call(
        functools.partial(sphere_kernel, tiles_high, tiles_wide),
        out_shape=jax.ShapeDtypeStruct((devices, cy, PARTS * cx), f32),
        in_specs=[SMEM, SMEM, VMEM],
        out_specs=VMEM,
        scratch_shapes=[
            pltpu.VMEM((2, 7, faces, side, width), f32),
            pltpu.VMEM((2, faces, side, width), f32),
            pltpu.VMEM((faces, side, width), f32),
            pltpu.VMEM((min(faces, 2), 7, side + 2 * PAD, width), f32),
            pltpu.VMEM((faces, 16, width), f32),
            pltpu.VMEM((faces, 16, width), f32),
        ],
        name="sphere",
    )(seam_partner.reshape(-1), seam_flip.reshape(-1), spheres)
    back = lax.all_to_all(result, AXES, 0, 0, tiled=True)
    return pl.pallas_call(
        unpack_kernel,
        out_shape=jax.ShapeDtypeStruct((cy, cx, lanes), f32),
        in_specs=[VMEM],
        out_specs=VMEM,
        name="unpack",
    )(back[:levels])[None]


def solution(mesh):
    placed = (
        P("face", "ty", "tx", None),
        P("face", "ty", "tx", None),
        P("face", "ty", "tx"),
        P("face", "ty", "tx", None),
        P("face", "ty", "tx"),
        P("face", "ty", "tx"),
        P(),
        P(),
    )
    return jax.shard_map(
        on_device,
        mesh=mesh,
        in_specs=placed,
        out_specs=P("face", "ty", "tx", None),
        check_vma=False,
    )
```

```python
import functools

import jax
import jax.numpy as jnp
from jax import lax
from jax.experimental import pallas as pl
from jax.experimental.pallas import tpu as pltpu
from jax.sharding import PartitionSpec as P

STEPS = 2
AXES = ("face", "ty", "tx")
PARTS = 4
PAD = 16
VMEM = pl.BlockSpec(memory_space=pltpu.VMEM)
SMEM = pl.BlockSpec(memory_space=pltpu.SMEM)


def loop(count, body):
    if count <= 8:
        for i in range(count):
            body(i)
    else:
        lax.fori_loop(0, count, lambda i, carry: (body(i), carry)[1], 0)


def split_parts(block, width, axis):
    return [lax.slice_in_dim(block, q * width, (q + 1) * width, axis=axis) for q in range(PARTS)]


def turned(block, rows):
    return jnp.concatenate(split_parts(block.T, rows, 0), axis=1)


def pack_kernel(cot_ref, cx_ref, ex_ref, cy_ref, ey_ref, area_ref, send_ref, rows_ref):
    cy, cx, lanes = cot_ref.shape
    levels = lanes // PARTS
    group = rows_ref.shape[1] // cx
    place = [
        pl.ds(pl.multiple_of((lax.axis_index("tx") + j) % group * cx, cx), cx) for j in range(3)
    ]
    area = area_ref[...]
    scale_x = [ex_ref[:, i : i + cx] / area for i in range(2)]
    scale_y = [ey_ref[:, i : i + cy] / area.T for i in range(2)]
    if group > 3:
        rows_ref[...] = jnp.zeros_like(rows_ref)

    by_x = []
    for x in range(cx):
        pieces = []
        for i in range(2):
            c = cx_ref[x + i]
            pieces += [c, c * scale_x[i][:, x : x + 1]]
        by_x.append(jnp.concatenate(pieces, axis=1))
    by_x = jnp.stack(by_x)
    for y0 in range(0, cy, 8):
        rows_ref[y0 : y0 + 8, place[1], :] = jnp.swapaxes(by_x[:, y0 : y0 + 8], 0, 1)
    for y in range(cy):
        pieces = []
        for i in range(2):
            c = cy_ref[y + i]
            pieces += [c, c * scale_y[i][:, y : y + 1]]
        rows_ref[y, place[2], :] = jnp.concatenate(pieces, axis=1)
        rows_ref[y, place[0], :] = cot_ref[y]
    for y in range(cy):
        send_ref[:, y, :] = turned(rows_ref[y], levels)


def unpack_kernel(recv_ref, out_ref, rows_ref):
    cy, cx, _ = out_ref.shape
    group = rows_ref.shape[1] // (PARTS * cx)
    place = lax.axis_index("tx") % group
    for y in range(cy):
        rows_ref[y] = recv_ref[:, y, :].T
        out_ref[y] = jnp.concatenate(
            [
                rows_ref[y, pl.ds(pl.multiple_of((q * group + place) * cx, cx), cx), :]
                for q in range(PARTS)
            ],
            axis=1,
        )


def stencil(coefs, side):
    c_low, f_low, c_high, f_high = (
        jnp.concatenate([part] * PARTS, axis=1) for part in split_parts(coefs, side, 1)
    )

    def interface(c, f):
        size = jnp.abs(c)
        half = 0.5 * size
        w = 3.0 * half * (1.0 - (2.0 / 3.0) * size)
        plus = c > 0
        centre = f * (1.0 - half - w)
        outer = f * (half - w)
        cell = f * (2.0 * w)
        zero = jnp.zeros_like(c)
        o_low, o_high = jnp.where(plus, outer, zero), jnp.where(plus, zero, outer)
        s_low, s_high = jnp.where(plus, cell, zero), jnp.where(plus, zero, cell)
        near, far = 7.0 / 12.0, 1.0 / 12.0
        return (
            -far * o_low,
            near * o_low - far * centre,
            near * (centre + o_low) - far * o_high + s_low,
            near * (centre + o_high) - far * o_low + s_high,
            near * o_high - far * centre,
            -far * o_high,
        )

    low, high = interface(c_low, f_low), interface(c_high, f_high)
    return (
        low[0],
        low[1] - high[0],
        low[2] - high[1],
        1.0 + low[3] - high[2],
        low[4] - high[3],
        low[5] - high[4],
        -high[5],
    )


def sphere_kernel(
    tiles_high, tiles_wide, partner_ref, flip_ref, recv_ref, out_ref, beta, acc, field, prod, rim
):
    faces, side, lanes = field.shape
    cy, cx = side // tiles_high, side // tiles_wide
    slots = prod.shape[0]
    slot_lanes = recv_ref.shape[2]
    group = slot_lanes // (PARTS * cx)
    span = group * cx
    lane_id = lax.broadcasted_iota(jnp.int32, (cy, slot_lanes), 1)
    place_id = lane_id // cx % group

    def row_block(i):
        f, ty = i // tiles_high, i % tiles_high
        start = ty * cy
        return f, pl.ds(start if isinstance(i, int) else pl.multiple_of(start, 8), cy)

    def assemble(i):
        f, rows = row_block(i)
        for j, target in enumerate((field, acc.at[0], acc.at[1])):
            blocks = []
            for first in range(0, tiles_wide, group):
                tiles = [recv_ref[i * tiles_wide + first + tx] for tx in range(group)]
                block = tiles[0]
                for tx in range(1, group):
                    block = jnp.where(place_id == (tx + j) % group, tiles[tx], block)
                if j:
                    ahead = pltpu.roll(block, slot_lanes - j * cx, 1)
                    around = pltpu.roll(block, span - j * cx, 1)
                    block = jnp.where(place_id < group - j, ahead, around)
                blocks.append(block)
            if len(blocks) == 1:
                value = blocks[0]
            else:
                value = jnp.concatenate(
                    [block[:, q * span : (q + 1) * span] for q in range(PARTS) for block in blocks],
                    axis=1,
                )
            target[f, rows, :] = value

    loop(faces * tiles_high, assemble)

    def coefficients(f):
        for k, value in enumerate(stencil(turned(acc[0, f], side), side)):
            beta[0, k, f] = value
        for k, value in enumerate(stencil(acc[1, f], side)):
            beta[1, k, f] = value

    loop(faces, coefficients)
    prod[...] = jnp.zeros_like(prod)
    rim[...] = jnp.zeros_like(rim)
    mirror_id = lax.broadcasted_iota(jnp.int32, (8, 128), 1)
    mirror_id = mirror_id // side * side + (side - 1 - mirror_id % side)

    def sweep(d):
        def apply(f):
            cells = field[f]
            here = prod.at[f % slots]
            total = None
            for k in range(7):
                here[k, PAD : PAD + side, :] = beta[d, k, f] * cells
            for k in range(7):
                start = PAD - 8 - (k - 3)
                term = here[k, start : start + side + 16, :]
                total = term if total is None else total + term
            acc[d, f] = total[8 : 8 + side]
            acc[1 - d, f] = jnp.zeros((side, lanes), jnp.float32)
            for low in range(2):
                rows = total[0:8] if low else total[side + 8 :]
                rim[0, low, f, low] = rows
                for depth in range(3):
                    source, target = (7 - depth, depth) if low else (depth, 7 - depth)
                    rim[0, 1 - low, f, low, target : target + 1, :] = rows[source : source + 1]
                for order in range(2):
                    value = rim[0, order, f, low]
                    rim[1, order, f, low] = jnp.concatenate(
                        [
                            jnp.take_along_axis(value[:, at : at + 128], mirror_id, axis=1)
                            for at in range(0, lanes, 128)
                        ],
                        axis=1,
                    )

        loop(faces, apply)
        for f in range(faces):
            for low in range(2):
                edge = d + 2 * low
                code = partner_ref[f, edge]
                other, border = code // 4, code % 4
                high = jnp.where(border < 2, 1, 0)
                rows = pl.ds(pl.multiple_of(high * (side - 8), 8), 8)
                layout = border % 2
                acc[layout, other, rows, :] = (
                    acc[layout, other, rows, :] + rim[flip_ref[f, edge], high, f, low]
                )

        def merge(f):
            field[f] = turned(acc[d, f], side) + acc[1 - d, f]

        loop(faces, merge)

    for step in range(STEPS):
        sweep(1)
        sweep(0)

    def hand_out(i):
        f, rows = row_block(i)
        block = field[f, rows, :]
        for first in range(0, tiles_wide, group):
            if group == tiles_wide:
                value = block
            else:
                value = jnp.concatenate(
                    [part[:, first * cx : first * cx + span] for part in split_parts(block, side, 1)],
                    axis=1,
                )
            for tx in range(first, first + group):
                out_ref[i * tiles_wide + tx] = value

    loop(faces * tiles_high, hand_out)


def grant(*blocks):
    words = sum(functools.reduce(lambda a, b: a * b, (*shape[:-2], -(-shape[-2] // 8) * 8, -(-shape[-1] // 128) * 128)) for shape in blocks)
    return pltpu.CompilerParams(vmem_limit_bytes=5 * words + (2 << 20))


def on_device(cotangent, courant_x, edge_x, courant_y, edge_y, cell_area, seam_partner, seam_flip):
    cells = cotangent[0]
    cy, cx, lanes = cells.shape
    levels = courant_x.shape[-1]
    faces, tiles_high, tiles_wide = (lax.axis_size(axis) for axis in AXES)
    devices = faces * tiles_high * tiles_wide
    side = cx * tiles_wide
    width = PARTS * side
    group = 128 // (PARTS * cx)
    if lanes != PARTS * levels or devices % levels or side != cy * tiles_high:
        raise ValueError("unsupported sizes")
    if cx % 8 or cy % 8 or group < 3 or tiles_wide % group or 128 % side:
        raise ValueError("unsupported tile")
    f32 = jnp.float32
    slot = PARTS * group * cx

    pack_rows = (cy, group * cx, lanes)
    send = pl.pallas_call(
        pack_kernel,
        out_shape=jax.ShapeDtypeStruct((levels, cy, slot), f32),
        in_specs=[VMEM] * 6,
        out_specs=VMEM,
        scratch_shapes=[pltpu.VMEM(pack_rows, f32)],
        compiler_params=grant(*[cells.shape] * 4, pack_rows, (levels, cy, slot)),
        name="pack",
    )(
        cells,
        jnp.swapaxes(courant_x[0], 0, 1),
        edge_x[0],
        courant_y[0],
        jnp.swapaxes(edge_y[0], 0, 1),
        cell_area[0],
    )
    if devices > levels:
        send = jnp.tile(send, (devices // levels, 1, 1))
    spheres = lax.all_to_all(send, AXES, 0, 0, tiled=True)
    scratch = [
        (2, 7, faces, side, width),
        (2, faces, side, width),
        (faces, side, width),
        (min(faces, 2), 7, side + 2 * PAD, width),
        (2, 2, faces, 2, 8, width),
    ]
    result = pl.pallas_call(
        functools.partial(sphere_kernel, tiles_high, tiles_wide),
        out_shape=jax.ShapeDtypeStruct((devices, cy, slot), f32),
        in_specs=[SMEM, SMEM, VMEM],
        out_specs=VMEM,
        scratch_shapes=[pltpu.VMEM(shape, f32) for shape in scratch],
        compiler_params=grant(*[(devices, cy, slot)] * 2, *scratch),
        name="sphere",
    )(seam_partner, seam_flip, spheres)
    back = lax.all_to_all(result, AXES, 0, 0, tiled=True)[:levels]
    unpack_rows = (cy, slot, levels)
    return pl.pallas_call(
        unpack_kernel,
        out_shape=jax.ShapeDtypeStruct((cy, cx, lanes), f32),
        in_specs=[VMEM],
        out_specs=VMEM,
        scratch_shapes=[pltpu.VMEM(unpack_rows, f32)],
        compiler_params=grant(cells.shape, back.shape, unpack_rows),
        name="unpack",
    )(back)[None]


def solution(mesh):
    placed = (
        P("face", "ty", "tx", None),
        P("face", "ty", "tx", None),
        P("face", "ty", "tx"),
        P("face", "ty", "tx", None),
        P("face", "ty", "tx"),
        P("face", "ty", "tx"),
        P(),
        P(),
    )
    return jax.shard_map(
        on_device,
        mesh=mesh,
        in_specs=placed,
        out_specs=P("face", "ty", "tx", None),
        check_vma=False,
    )
```

```python
import functools

import jax
import jax.numpy as jnp
from jax import lax
from jax.experimental import pallas as pl
from jax.experimental.pallas import tpu as pltpu
from jax.sharding import PartitionSpec as P

STEPS = 2
AXES = ("ty", "face", "tx")
PARTS = 4
PAD = 16
VMEM = pl.BlockSpec(memory_space=pltpu.VMEM)
SMEM = pl.BlockSpec(memory_space=pltpu.SMEM)
HBM = pl.BlockSpec(memory_space=pltpu.HBM)


def loop(count, body):
    if count <= 8:
        for i in range(count):
            body(i)
    else:
        lax.fori_loop(0, count, lambda i, carry: (body(i), carry)[1], 0)


def split_parts(block, width, axis):
    return [lax.slice_in_dim(block, q * width, (q + 1) * width, axis=axis) for q in range(PARTS)]


def turned(block, rows):
    return jnp.concatenate(split_parts(block.T, rows, 0), axis=1)


def pack_kernel(*refs):
    sources, send_ref, rows_ref, sems = refs[:6], refs[6], refs[7], refs[14]
    cot_ref, cx_ref, ex_ref, cy_ref, ey_ref, area_ref = refs[8:14]
    copies = [
        pltpu.make_async_copy(source, target, sems.at[i])
        for i, (source, target) in enumerate(zip(sources, refs[8:14]))
    ]
    for copy in copies:
        copy.start()
    cy, cx, lanes = cot_ref.shape
    levels = lanes // PARTS
    group = rows_ref.shape[1] // cx
    place = [
        pl.ds(pl.multiple_of((lax.axis_index("tx") + j) % group * cx, cx), cx) for j in range(3)
    ]
    for copy in copies:
        copy.wait()
    area = area_ref[...]
    scale_x = [ex_ref[:, i : i + cx] / area for i in range(2)]
    scale_y = [ey_ref[:, i : i + cy] / area.T for i in range(2)]
    if group > 3:
        rows_ref[...] = jnp.zeros_like(rows_ref)

    by_x = []
    for x in range(cx):
        pieces = []
        for i in range(2):
            c = cx_ref[x + i]
            pieces += [c, c * scale_x[i][:, x : x + 1]]
        by_x.append(jnp.concatenate(pieces, axis=1))
    by_x = jnp.stack(by_x)
    for y0 in range(0, cy, 8):
        rows_ref[y0 : y0 + 8, place[1], :] = jnp.swapaxes(by_x[:, y0 : y0 + 8], 0, 1)
    for y in range(cy):
        pieces = []
        for i in range(2):
            c = cy_ref[y + i]
            pieces += [c, c * scale_y[i][:, y : y + 1]]
        rows_ref[y, place[2], :] = jnp.concatenate(pieces, axis=1)
        rows_ref[y, place[0], :] = cot_ref[y]
    for y in range(cy):
        send_ref[:, y, :] = turned(rows_ref[y], levels)


def unpack_kernel(recv_ref, out_ref):
    cy, cx, lanes = out_ref.shape
    levels = lanes // PARTS
    group = 128 // (PARTS * cx)
    half = 8 // group
    count = cy // group
    for r in range(count):
        block = recv_ref[pl.ds(r, levels, stride=count), :].T
        for b in range(group):
            out_ref[r // half * 8 + b * half + r % half] = jnp.concatenate(
                [block[(q * group + b) * cx : (q * group + b + 1) * cx] for q in range(PARTS)], axis=1
            )


def stencil(coefs, side):
    c_low, f_low, c_high, f_high = (
        jnp.concatenate([part] * PARTS, axis=1) for part in split_parts(coefs, side, 1)
    )

    def interface(c, f):
        size = jnp.abs(c)
        half = 0.5 * size
        w = 3.0 * half * (1.0 - (2.0 / 3.0) * size)
        plus = c > 0
        centre = f * (1.0 - half - w)
        outer = f * (half - w)
        cell = f * (2.0 * w)
        zero = jnp.zeros_like(c)
        o_low, o_high = jnp.where(plus, outer, zero), jnp.where(plus, zero, outer)
        s_low, s_high = jnp.where(plus, cell, zero), jnp.where(plus, zero, cell)
        near, far = 7.0 / 12.0, 1.0 / 12.0
        return (
            -far * o_low,
            near * o_low - far * centre,
            near * (centre + o_low) - far * o_high + s_low,
            near * (centre + o_high) - far * o_low + s_high,
            near * o_high - far * centre,
            -far * o_high,
        )

    low, high = interface(c_low, f_low), interface(c_high, f_high)
    return (
        low[0],
        low[1] - high[0],
        low[2] - high[1],
        1.0 + low[3] - high[2],
        low[4] - high[3],
        low[5] - high[4],
        -high[5],
    )


def sphere_kernel(
    tiles_high, tiles_wide, partner_ref, flip_ref, recv_ref, out_ref, beta, acc, field, prod, rim
):
    faces, side, lanes = field.shape
    cy, cx = side // tiles_high, side // tiles_wide
    slots = prod.shape[0]
    slot_lanes = recv_ref.shape[2]
    group = slot_lanes // (PARTS * cx)
    span = group * cx
    lane_id = lax.broadcasted_iota(jnp.int32, (cy, slot_lanes), 1)
    place_id = lane_id // cx % group

    def row_block(i):
        f, ty = i % faces, i // faces
        start = ty * cy
        return f, pl.ds(start if isinstance(i, int) else pl.multiple_of(start, 8), cy)

    def assemble(i):
        f, rows = row_block(i)
        for j, target in enumerate((field, acc.at[0], acc.at[1])):
            blocks = []
            for first in range(0, tiles_wide, group):
                tiles = [recv_ref[i * tiles_wide + first + tx] for tx in range(group)]
                block = tiles[0]
                for tx in range(1, group):
                    block = jnp.where(place_id == (tx + j) % group, tiles[tx], block)
                if j:
                    ahead = pltpu.roll(block, slot_lanes - j * cx, 1)
                    around = pltpu.roll(block, span - j * cx, 1)
                    block = jnp.where(place_id < group - j, ahead, around)
                blocks.append(block)
            if len(blocks) == 1:
                value = blocks[0]
            else:
                value = jnp.concatenate(
                    [block[:, q * span : (q + 1) * span] for q in range(PARTS) for block in blocks],
                    axis=1,
                )
            target[f, rows, :] = value

    loop(faces * tiles_high, assemble)

    def coefficients(f):
        for k, value in enumerate(stencil(turned(acc[0, f], side), side)):
            beta[0, k, f] = value
        for k, value in enumerate(stencil(acc[1, f], side)):
            beta[1, k, f] = value

    loop(faces, coefficients)
    prod[...] = jnp.zeros_like(prod)
    rim[...] = jnp.zeros_like(rim)
    mirror_id = lax.broadcasted_iota(jnp.int32, (8, 128), 1)
    mirror_id = mirror_id // side * side + (side - 1 - mirror_id % side)

    def sweep(d):
        def apply(f):
            cells = field[f]
            here = prod.at[f % slots]
            total = None
            for k in range(7):
                here[k, PAD : PAD + side, :] = beta[d, k, f] * cells
            for k in range(7):
                start = PAD - 8 - (k - 3)
                term = here[k, start : start + side + 16, :]
                total = term if total is None else total + term
            acc[d, f] = total[8 : 8 + side]
            acc[1 - d, f] = jnp.zeros((side, lanes), jnp.float32)
            for low in range(2):
                rows = total[0:8] if low else total[side + 8 :]
                rim[0, low, f, low] = rows
                for depth in range(3):
                    source, target = (7 - depth, depth) if low else (depth, 7 - depth)
                    rim[0, 1 - low, f, low, target : target + 1, :] = rows[source : source + 1]
                for order in range(2):
                    value = rim[0, order, f, low]
                    rim[1, order, f, low] = jnp.concatenate(
                        [
                            jnp.take_along_axis(value[:, at : at + 128], mirror_id, axis=1)
                            for at in range(0, lanes, 128)
                        ],
                        axis=1,
                    )

        loop(faces, apply)
        for f in range(faces):
            for low in range(2):
                edge = d + 2 * low
                code = partner_ref[f, edge]
                other, border = code // 4, code % 4
                high = jnp.where(border < 2, 1, 0)
                rows = pl.ds(pl.multiple_of(high * (side - 8), 8), 8)
                layout = border % 2
                acc[layout, other, rows, :] = (
                    acc[layout, other, rows, :] + rim[flip_ref[f, edge], high, f, low]
                )

        def merge(f):
            field[f] = turned(acc[d, f], side) + acc[1 - d, f]

        loop(faces, merge)

    for step in range(STEPS):
        sweep(1)
        sweep(0)

    half = 8 // group
    row_id = lax.broadcasted_iota(jnp.int32, (8, slot_lanes), 0) // half
    place = lax.broadcasted_iota(jnp.int32, (8, slot_lanes), 1) // cx % group

    def tiles_to_rows(block):
        bit = 1
        while bit < group:
            down = pltpu.roll(pltpu.roll(block, 8 - half * bit, 0), bit * cx, 1)
            up = pltpu.roll(pltpu.roll(block, half * bit, 0), slot_lanes - bit * cx, 1)
            a, b = row_id // bit % 2, place // bit % 2
            block = jnp.where(a == b, block, jnp.where(a == 0, down, up))
            bit *= 2
        return block

    count = cy // group

    def hand_out(i):
        f, rows = row_block(i)
        strip = field[f, rows, :]
        for part in range(0, cy, 8):
            block = strip[part : part + 8]
            for first in range(0, tiles_wide, group):
                if group == tiles_wide:
                    value = block
                else:
                    value = jnp.concatenate(
                        [piece[:, first * cx : first * cx + span] for piece in split_parts(block, side, 1)],
                        axis=1,
                    )
                value = tiles_to_rows(value)
                base = (i * tiles_wide + first) * count
                if cy == 8:
                    out_ref[pl.ds(base if isinstance(i, int) else pl.multiple_of(base, 8), 8), :] = value
                else:
                    for a in range(group):
                        out_ref[pl.ds(base + a * count + part // 8 * half, half), :] = value[a * half : (a + 1) * half]

    loop(faces * tiles_high, hand_out)


def grant(*blocks):
    words = sum(functools.reduce(lambda a, b: a * b, (*shape[:-2], -(-shape[-2] // 8) * 8, -(-shape[-1] // 128) * 128)) for shape in blocks)
    return pltpu.CompilerParams(vmem_limit_bytes=5 * words + (2 << 20))


def on_device(cotangent, courant_x, edge_x, courant_y, edge_y, cell_area, seam_partner, seam_flip):
    cells = cotangent[0]
    cy, cx, lanes = cells.shape
    levels = courant_x.shape[-1]
    faces, tiles_high, tiles_wide = (lax.axis_size(axis) for axis in ("face", "ty", "tx"))
    devices = faces * tiles_high * tiles_wide
    side = cx * tiles_wide
    width = PARTS * side
    group = 128 // (PARTS * cx)
    if lanes != PARTS * levels or devices % levels or side != cy * tiles_high:
        raise ValueError("unsupported sizes")
    if cx % 8 or cy % 8 or group != 4 or tiles_wide % group or 128 % side:
        raise ValueError("unsupported tile")
    f32 = jnp.float32
    slot = PARTS * group * cx

    arguments = (
        cells,
        jnp.swapaxes(courant_x[0], 0, 1),
        edge_x[0],
        courant_y[0],
        jnp.swapaxes(edge_y[0], 0, 1),
        cell_area[0],
    )
    pack_rows = (cy, group * cx, lanes)
    send = pl.pallas_call(
        pack_kernel,
        out_shape=jax.ShapeDtypeStruct((levels, cy, slot), f32),
        in_specs=[HBM] * 6,
        out_specs=VMEM,
        scratch_shapes=[
            pltpu.VMEM(pack_rows, f32),
            *[pltpu.VMEM(argument.shape, f32) for argument in arguments],
            pltpu.SemaphoreType.DMA((6,)),
        ],
        compiler_params=grant(*[cells.shape] * 4, pack_rows, (levels, cy, slot)),
        name="pack",
    )(*(pltpu.with_memory_space_constraint(argument, pltpu.HBM) for argument in arguments))
    if devices > levels:
        send = jnp.tile(send, (devices // levels, 1, 1))
    spheres = lax.all_to_all(send, AXES, 0, 0, tiled=True)
    scratch = [
        (2, 7, faces, side, width),
        (2, faces, side, width),
        (faces, side, width),
        (min(faces, 2), 7, side + 2 * PAD, width),
        (2, 2, faces, 2, 8, width),
    ]
    back = (devices * cy // group, slot)
    result = pl.pallas_call(
        functools.partial(sphere_kernel, tiles_high, tiles_wide),
        out_shape=jax.ShapeDtypeStruct(back, f32),
        in_specs=[SMEM, SMEM, VMEM],
        out_specs=VMEM,
        scratch_shapes=[pltpu.VMEM(shape, f32) for shape in scratch],
        compiler_params=grant((devices, cy, slot), back, *scratch),
        name="sphere",
    )(seam_partner, seam_flip, spheres)
    strips = lax.all_to_all(result, AXES, 0, 0, tiled=True)[: levels * cy // group]
    return pl.pallas_call(
        unpack_kernel,
        out_shape=jax.ShapeDtypeStruct(cells.shape, f32),
        in_specs=[VMEM],
        out_specs=VMEM,
        compiler_params=grant(cells.shape, strips.shape),
        name="unpack",
    )(strips)[None]


def solution(mesh):
    placed = (
        P("face", "ty", "tx", None),
        P("face", "ty", "tx", None),
        P("face", "ty", "tx"),
        P("face", "ty", "tx", None),
        P("face", "ty", "tx"),
        P("face", "ty", "tx"),
        P(),
        P(),
    )
    return jax.shard_map(
        on_device,
        mesh=mesh,
        in_specs=placed,
        out_specs=P("face", "ty", "tx", None),
        check_vma=False,
    )
```

```python
import functools
import math

import jax
import jax.numpy as jnp
from jax import lax
from jax.experimental import pallas as pl
from jax.experimental.pallas import tpu as pltpu
from jax.sharding import PartitionSpec as P

STEPS = 2
AXES = ("ty", "face", "tx")
PARTS = 4
PAD = 16
VMEM = pl.BlockSpec(memory_space=pltpu.VMEM)
HBM = pl.BlockSpec(memory_space=pltpu.HBM)


def loop(count, body):
    if count <= 8:
        for i in range(count):
            body(i)
    else:
        lax.fori_loop(0, count, lambda i, carry: (body(i), carry)[1], 0)


def split_parts(block, width, axis):
    return [lax.slice_in_dim(block, q * width, (q + 1) * width, axis=axis) for q in range(PARTS)]


def turned(block, rows):
    return jnp.concatenate(split_parts(block.T, rows, 0), axis=1)


def pack_kernel(*refs):
    sources, send_ref, rows_ref, sems = refs[:6], refs[6], refs[7], refs[14]
    cot_ref, cx_ref, ex_ref, cy_ref, ey_ref, area_ref = refs[8:14]
    copies = [
        pltpu.make_async_copy(source, target, sems.at[i])
        for i, (source, target) in enumerate(zip(sources, refs[8:14]))
    ]
    for copy in copies:
        copy.start()
    cy, cx, lanes = cot_ref.shape
    levels = lanes // PARTS
    group = 128 // (PARTS * cx)
    span = group * cx
    place = [pl.multiple_of(((lax.axis_index("tx") + j) & (group - 1)) * cx, cx) for j in range(3)]
    for copy in copies:
        copy.wait()
    area = area_ref[...]
    scale_x = [ex_ref[:, i : i + cx] / area for i in range(2)]
    scale_y = [ey_ref[:, i : i + cy] / area.T for i in range(2)]

    for x in range(cx):
        pieces = []
        for i in range(2):
            c = cx_ref[x + i]
            pieces += [c, c * scale_x[i][:, x : x + 1]]
        rows_ref[pl.ds(place[1] + x, cy, stride=span), :] = jnp.concatenate(pieces, axis=1)
    for y in range(cy):
        pieces = []
        for i in range(2):
            c = cy_ref[y + i]
            pieces += [c, c * scale_y[i][:, y : y + 1]]
        rows_ref[pl.ds(y * span + place[2], cx), :] = jnp.concatenate(pieces, axis=1)
        rows_ref[pl.ds(y * span + place[0], cx), :] = cot_ref[y]
    for y in range(cy):
        send_ref[pl.ds(y, levels, stride=cy), :] = turned(rows_ref[y * span : (y + 1) * span], levels)


def unpack_kernel(recv_ref, out_ref):
    cy, cx, lanes = out_ref.shape
    levels = lanes // PARTS
    group = 128 // (PARTS * cx)
    half = 8 // group
    count = cy // group
    for r in range(count):
        block = recv_ref[pl.ds(r, levels, stride=count), :].T
        for b in range(group):
            out_ref[r // half * 8 + b * half + r % half] = jnp.concatenate(
                [block[(q * group + b) * cx : (q * group + b + 1) * cx] for q in range(PARTS)], axis=1
            )


def stencil(coefs, side):
    c_low, f_low, c_high, f_high = (
        jnp.concatenate([part] * PARTS, axis=1) for part in split_parts(coefs, side, 1)
    )

    def interface(c, f):
        size = jnp.abs(c)
        half = 0.5 * size
        w = 3.0 * half * (1.0 - (2.0 / 3.0) * size)
        plus = c > 0
        centre = f * (1.0 - half - w)
        outer = f * (half - w)
        cell = f * (2.0 * w)
        zero = jnp.zeros_like(c)
        o_low, o_high = jnp.where(plus, outer, zero), jnp.where(plus, zero, outer)
        s_low, s_high = jnp.where(plus, cell, zero), jnp.where(plus, zero, cell)
        near, far = 7.0 / 12.0, 1.0 / 12.0
        return (
            -far * o_low,
            near * o_low - far * centre,
            near * (centre + o_low) - far * o_high + s_low,
            near * (centre + o_high) - far * o_low + s_high,
            near * o_high - far * centre,
            -far * o_high,
        )

    low, high = interface(c_low, f_low), interface(c_high, f_high)
    return (
        low[0],
        low[1] - high[0],
        low[2] - high[1],
        1.0 + low[3] - high[2],
        low[4] - high[3],
        low[5] - high[4],
        -high[5],
    )


def sphere_kernel(
    tiles_high,
    tiles_wide,
    partner_hbm,
    flip_hbm,
    recv_ref,
    out_ref,
    beta,
    acc,
    field,
    prod,
    rim,
    partner_ref,
    flip_ref,
    sems,
):
    copies = [
        pltpu.make_async_copy(partner_hbm, partner_ref, sems.at[0]),
        pltpu.make_async_copy(flip_hbm, flip_ref, sems.at[1]),
    ]
    for copy in copies:
        copy.start()
    faces, side, lanes = field.shape
    cy, cx = side // tiles_high, side // tiles_wide
    slots = prod.shape[0]
    slot_lanes = recv_ref.shape[2]
    group = slot_lanes // (PARTS * cx)
    span = group * cx
    lane_id = lax.broadcasted_iota(jnp.int32, (cy, slot_lanes), 1)
    place_id = (lane_id >> (cx.bit_length() - 1)) & (group - 1)

    def row_block(i):
        f, ty = i % faces, i // faces
        start = ty * cy
        return f, pl.ds(start if isinstance(i, int) else pl.multiple_of(start, 8), cy)

    def assemble(i):
        f, rows = row_block(i)
        for j, target in enumerate((field, acc.at[0], acc.at[1])):
            blocks = []
            for first in range(0, tiles_wide, group):
                tiles = [recv_ref[i * tiles_wide + first + tx] for tx in range(group)]
                block = tiles[0]
                for tx in range(1, group):
                    block = jnp.where(place_id == (tx + j) % group, tiles[tx], block)
                if j:
                    ahead = pltpu.roll(block, slot_lanes - j * cx, 1)
                    around = pltpu.roll(block, span - j * cx, 1)
                    block = jnp.where(place_id < group - j, ahead, around)
                blocks.append(block)
            if len(blocks) == 1:
                value = blocks[0]
            else:
                value = jnp.concatenate(
                    [block[:, q * span : (q + 1) * span] for q in range(PARTS) for block in blocks],
                    axis=1,
                )
            target[f, rows, :] = value

    loop(faces * tiles_high, assemble)

    def coefficients(f):
        for k, value in enumerate(stencil(turned(acc[0, f], side), side)):
            beta[0, k, f] = value
        for k, value in enumerate(stencil(acc[1, f], side)):
            beta[1, k, f] = value

    loop(faces, coefficients)
    prod[...] = jnp.zeros_like(prod)
    rim[...] = jnp.zeros_like(rim)
    mirror_id = lax.broadcasted_iota(jnp.int32, (8, 128), 1)
    mirror_id = mirror_id ^ (side - 1)
    upside_id = 7 - lax.broadcasted_iota(jnp.int32, (8, 128), 0)

    def by_lanes(fun, value):
        return jnp.concatenate([fun(value[:, at : at + 128]) for at in range(0, lanes, 128)], axis=1)

    def mirrored(value):
        return by_lanes(lambda chunk: jnp.take_along_axis(chunk, mirror_id, axis=1), value)

    def upside(value):
        return by_lanes(lambda chunk: jnp.take_along_axis(chunk, upside_id, axis=0), value)

    for copy in copies:
        copy.wait()

    def sweep(d):
        def apply(f):
            cells = field[f]
            here = prod.at[f % slots]
            middle = beta[d, 3, f] * cells
            for k in range(7):
                if k != 3:
                    here[k, PAD : PAD + side, :] = beta[d, k, f] * cells
            before, after = None, None
            for k in (0, 1, 2, 4, 5, 6):
                shift = k - 3
                middle = middle + here[k, PAD - shift : PAD - shift + side, :]
                if shift < 0:
                    term = here[k, PAD - 8 - shift : PAD - shift, :]
                    before = term if before is None else before + term
                else:
                    term = here[k, PAD + side - shift : PAD + side + 8 - shift, :]
                    after = term if after is None else after + term
            acc[0, f] = middle
            for low, rows in ((0, after), (1, before)):
                orders = (rows, upside(rows))
                for order in range(2):
                    value = orders[order ^ low]
                    rim[0, order, f, low] = value
                    rim[1, order, f, low] = mirrored(value)

        loop(faces, apply)

        def seam(f, edge):
            code = partner_ref[f, edge]
            value = rim[flip_ref[f, edge], int(edge < 2), code >> 2, (code & 3) >> 1]
            return jnp.where((code & 1) == d, value, 0.0)

        def with_seams(value, f, axis):
            return jnp.concatenate(
                [
                    value[0:8] + seam(f, axis + 2),
                    value[8 : side - 8],
                    value[side - 8 :] + seam(f, axis),
                ],
                axis=0,
            )

        if faces * side <= 128:
            block = jnp.concatenate([with_seams(acc[0, f], f, d) for f in range(faces)], axis=0).T
            for f in range(faces):
                columns = block[:, f * side : (f + 1) * side]
                value = jnp.concatenate(split_parts(columns, side, 0), axis=1)
                field[f] = with_seams(value, f, 1 - d)
        else:

            def merge(f):
                field[f] = with_seams(turned(with_seams(acc[0, f], f, d), side), f, 1 - d)

            loop(faces, merge)

    for step in range(STEPS):
        sweep(1)
        sweep(0)

    half = 8 // group
    row_id = lax.broadcasted_iota(jnp.int32, (8, slot_lanes), 0) >> (half.bit_length() - 1)
    place = place_id[0:8]

    def tiles_to_rows(block):
        bit = 1
        while bit < group:
            down = pltpu.roll(pltpu.roll(block, 8 - half * bit, 0), bit * cx, 1)
            up = pltpu.roll(pltpu.roll(block, half * bit, 0), slot_lanes - bit * cx, 1)
            a, b = row_id & bit, place & bit
            block = jnp.where(a == b, block, jnp.where(a == 0, down, up))
            bit *= 2
        return block

    count = cy // group

    def hand_out(i):
        f, rows = row_block(i)
        strip = field[f, rows, :]
        for part in range(0, cy, 8):
            block = strip[part : part + 8]
            for first in range(0, tiles_wide, group):
                if group == tiles_wide:
                    value = block
                else:
                    value = jnp.concatenate(
                        [piece[:, first * cx : first * cx + span] for piece in split_parts(block, side, 1)],
                        axis=1,
                    )
                value = tiles_to_rows(value)
                base = (i * tiles_wide + first) * count
                if cy == 8:
                    out_ref[pl.ds(base if isinstance(i, int) else pl.multiple_of(base, 8), 8), :] = value
                else:
                    for a in range(group):
                        out_ref[pl.ds(base + a * count + part // 8 * half, half), :] = value[a * half : (a + 1) * half]

    loop(faces * tiles_high, hand_out)


def in_hbm(array):
    return pltpu.with_memory_space_constraint(array, pltpu.HBM)


def grant(*shapes):
    size = 0
    for *major, rows, columns in shapes:
        size += 4 * math.prod(major) * (-(-rows // 8) * 8) * (-(-columns // 128) * 128)
    return pltpu.CompilerParams(vmem_limit_bytes=size + size // 4 + (2 << 20))


def on_device(cotangent, courant_x, edge_x, courant_y, edge_y, cell_area, seam_partner, seam_flip):
    cells = cotangent[0]
    cy, cx, lanes = cells.shape
    levels = courant_x.shape[-1]
    faces, tiles_high, tiles_wide = (lax.axis_size(axis) for axis in ("face", "ty", "tx"))
    devices = faces * tiles_high * tiles_wide
    side = cx * tiles_wide
    width = PARTS * side
    group = 128 // (PARTS * cx)
    if lanes != PARTS * levels or devices % levels or side != cy * tiles_high:
        raise ValueError("unsupported sizes")
    if cx != 8 or cy % 8 or tiles_wide % group or 128 % side:
        raise ValueError("unsupported tile")
    f32 = jnp.float32
    slot = PARTS * group * cx

    arguments = (
        cells,
        jnp.swapaxes(courant_x[0], 0, 1),
        edge_x[0],
        courant_y[0],
        jnp.swapaxes(edge_y[0], 0, 1),
        cell_area[0],
    )
    pack_rows = (cy * group * cx, lanes)
    send = pl.pallas_call(
        pack_kernel,
        out_shape=jax.ShapeDtypeStruct((levels * cy, slot), f32),
        in_specs=[HBM] * 6,
        out_specs=VMEM,
        scratch_shapes=[
            pltpu.VMEM(pack_rows, f32),
            *[pltpu.VMEM(argument.shape, f32) for argument in arguments],
            pltpu.SemaphoreType.DMA((6,)),
        ],
        compiler_params=grant(*[cells.shape] * 4, pack_rows, (levels, cy, slot)),
        name="pack",
    )(*map(in_hbm, arguments))
    if devices > levels:
        send = jnp.tile(send, (devices // levels, 1))
    spheres = lax.all_to_all(send.reshape(devices, cy, slot), AXES, 0, 0, tiled=True)
    scratch = [
        (2, 7, faces, side, width),
        (2, faces, side, width),
        (faces, side, width),
        (min(faces, 2), 7, side + 2 * PAD, width),
        (2, 2, faces, 2, 8, width),
    ]
    back = (devices * cy // group, slot)
    result = pl.pallas_call(
        functools.partial(sphere_kernel, tiles_high, tiles_wide),
        out_shape=jax.ShapeDtypeStruct(back, f32),
        in_specs=[HBM, HBM, VMEM],
        out_specs=VMEM,
        scratch_shapes=[
            *[pltpu.VMEM(shape, f32) for shape in scratch],
            pltpu.SMEM(seam_partner.shape, jnp.int32),
            pltpu.SMEM(seam_flip.shape, jnp.int32),
            pltpu.SemaphoreType.DMA((2,)),
        ],
        compiler_params=grant((devices, cy, slot), back, *scratch),
        name="sphere",
    )(in_hbm(seam_partner), in_hbm(seam_flip), spheres)
    strips = lax.all_to_all(result, AXES, 0, 0, tiled=True)[: levels * cy // group]
    return pl.pallas_call(
        unpack_kernel,
        out_shape=jax.ShapeDtypeStruct(cells.shape, f32),
        in_specs=[VMEM],
        out_specs=VMEM,
        compiler_params=grant(cells.shape, strips.shape),
        name="unpack",
    )(strips)[None]


def solution(mesh):
    placed = (
        P("face", "ty", "tx", None),
        P("face", "ty", "tx", None),
        P("face", "ty", "tx"),
        P("face", "ty", "tx", None),
        P("face", "ty", "tx"),
        P("face", "ty", "tx"),
        P(),
        P(),
    )
    return jax.shard_map(
        on_device,
        mesh=mesh,
        in_specs=placed,
        out_specs=P("face", "ty", "tx", None),
        check_vma=False,
    )
```

```python
import functools
import math

import jax
import jax.numpy as jnp
from jax import lax
from jax.experimental import pallas as pl
from jax.experimental.pallas import tpu as pltpu
from jax.sharding import PartitionSpec as P

STEPS = 2
AXES = ("ty", "face", "tx")
PARTS = 4
PAD = 16
VMEM = pl.BlockSpec(memory_space=pltpu.VMEM)
HBM = pl.BlockSpec(memory_space=pltpu.HBM)


def loop(count, body):
    if count <= 8:
        for i in range(count):
            body(i)
    else:
        lax.fori_loop(0, count, lambda i, carry: (body(i), carry)[1], 0)


def split_parts(block, width, axis):
    return [lax.slice_in_dim(block, q * width, (q + 1) * width, axis=axis) for q in range(PARTS)]


def turned(block, rows):
    return jnp.concatenate(split_parts(block.T, rows, 0), axis=1)


def pack_kernel(
    cot_hbm, cx_hbm, ex_hbm, cy_hbm, ey_hbm, area_hbm, send_ref, rows_ref, cx_ref, ex_ref, cy_ref, ey_ref, area_ref, sems
):
    cy, cx = area_ref.shape
    lanes = rows_ref.shape[1]
    levels = lanes // PARTS
    group = 128 // (PARTS * cx)
    span = group * cx
    place = [pl.multiple_of(((lax.axis_index("tx") + j) & (group - 1)) * cx, cx) for j in range(3)]
    copies = [
        pltpu.make_async_copy(source, target, sems.at[i])
        for i, (source, target) in enumerate(
            [(ex_hbm, ex_ref), (ey_hbm, ey_ref), (area_hbm, area_ref), (cx_hbm, cx_ref), (cy_hbm, cy_ref)]
            + [(cot_hbm.at[y], rows_ref.at[pl.ds(y * span + place[0], cx)]) for y in range(cy)]
        )
    ]
    for copy in copies:
        copy.start()
    for copy in copies:
        copy.wait()

    for x in range(cx):
        rows_ref[pl.ds(place[1] + x, cy, stride=span), 0 : 2 * levels] = jnp.concatenate(
            [cx_ref[x], cx_ref[x + 1]], axis=1
        )
    for y in range(cy):
        rows_ref[pl.ds(y * span + place[1], cx), 2 * levels :] = jnp.concatenate(
            [cy_ref[y], cy_ref[y + 1]], axis=1
        )

    area = area_ref[...]
    ey = ey_ref[...].T
    gap = jnp.zeros((cy, span - cx), jnp.float32)
    metric = []
    for length in (ex_ref[:, 0:cx], ex_ref[:, 1 : cx + 1], ey[0:cy], ey[1 : cy + 1]):
        metric += [length / area, gap]
    metric = pltpu.roll(jnp.concatenate(metric, axis=1), place[2], 1)
    lane_id = lax.broadcasted_iota(jnp.int32, (levels, lanes), 1)
    here = (lane_id & (span - 1)) >> (cx.bit_length() - 1) == place[2] >> (cx.bit_length() - 1)

    for first in range(0, cy, group):
        block = rows_ref[first * span : (first + group) * span].T
        for i in range(group):
            y = first + i
            row = jnp.concatenate(
                [block[q * levels : (q + 1) * levels, i * span : (i + 1) * span] for q in range(PARTS)],
                axis=1,
            )
            send_ref[pl.ds(y, levels, stride=cy), :] = jnp.where(here, metric[y : y + 1], row)


def unpack_kernel(recv_ref, out_ref):
    cy, cx, lanes = out_ref.shape
    levels = lanes // PARTS
    group = 128 // (PARTS * cx)
    half = 8 // group
    count = cy // group
    for r in range(count):
        block = recv_ref[pl.ds(r, levels, stride=count), :].T
        for b in range(group):
            out_ref[r // half * 8 + b * half + r % half] = jnp.concatenate(
                [block[(q * group + b) * cx : (q * group + b + 1) * cx] for q in range(PARTS)], axis=1
            )


def stencil(*parts):
    c_low, f_low, c_high, f_high = (jnp.concatenate([part] * PARTS, axis=1) for part in parts)

    def interface(c, f):
        size = jnp.abs(c)
        half = 0.5 * size
        w = 3.0 * half * (1.0 - (2.0 / 3.0) * size)
        plus = c > 0
        centre = f * (1.0 - half - w)
        outer = f * (half - w)
        cell = f * (2.0 * w)
        zero = jnp.zeros_like(c)
        o_low, o_high = jnp.where(plus, outer, zero), jnp.where(plus, zero, outer)
        s_low, s_high = jnp.where(plus, cell, zero), jnp.where(plus, zero, cell)
        near, far = 7.0 / 12.0, 1.0 / 12.0
        return (
            -far * o_low,
            near * o_low - far * centre,
            near * (centre + o_low) - far * o_high + s_low,
            near * (centre + o_high) - far * o_low + s_high,
            near * o_high - far * centre,
            -far * o_high,
        )

    low, high = interface(c_low, f_low), interface(c_high, f_high)
    return (
        low[0],
        low[1] - high[0],
        low[2] - high[1],
        1.0 + low[3] - high[2],
        low[4] - high[3],
        low[5] - high[4],
        -high[5],
    )


def sphere_kernel(
    tiles_high,
    tiles_wide,
    partner_hbm,
    flip_hbm,
    recv_ref,
    out_ref,
    beta,
    coef,
    acc,
    field,
    prod,
    rim,
    partner_ref,
    flip_ref,
    sems,
):
    copies = [
        pltpu.make_async_copy(partner_hbm, partner_ref, sems.at[0]),
        pltpu.make_async_copy(flip_hbm, flip_ref, sems.at[1]),
    ]
    for copy in copies:
        copy.start()
    faces, side, lanes = field.shape
    cy, cx = side // tiles_high, side // tiles_wide
    slots = prod.shape[0]
    slot_lanes = recv_ref.shape[2]
    group = slot_lanes // (PARTS * cx)
    span = group * cx
    lane_id = lax.broadcasted_iota(jnp.int32, (cy, slot_lanes), 1)
    place_id = (lane_id >> (cx.bit_length() - 1)) & (group - 1)

    def row_block(i):
        f, ty = i % faces, i // faces
        start = ty * cy
        return f, pl.ds(start if isinstance(i, int) else pl.multiple_of(start, 8), cy)

    def assemble(i):
        f, rows = row_block(i)
        values = []
        for j in range(3):
            blocks = []
            for first in range(0, tiles_wide, group):
                tiles = [recv_ref[i * tiles_wide + first + tx] for tx in range(group)]
                block = tiles[0]
                for tx in range(1, group):
                    block = jnp.where(place_id == (tx + j) % group, tiles[tx], block)
                if j:
                    ahead = pltpu.roll(block, slot_lanes - j * cx, 1)
                    around = pltpu.roll(block, span - j * cx, 1)
                    block = jnp.where(place_id < group - j, ahead, around)
                blocks.append(block)
            if len(blocks) == 1:
                values.append(blocks[0])
            else:
                values.append(
                    jnp.concatenate(
                        [block[:, q * span : (q + 1) * span] for q in range(PARTS) for block in blocks],
                        axis=1,
                    )
                )
        cells, courant, metric = values
        field[f, rows, :] = cells
        coef[0, f, rows, :] = courant
        coef[1, f, rows, :] = courant * metric

    loop(faces * tiles_high, assemble)

    def over_groups(body):
        if faces * side <= 128:
            body(list(range(faces)))
        else:
            loop(faces, lambda f: body([f]))

    def turned_parts(blocks):
        if len(blocks) == 1:
            return [split_parts(blocks[0].T, side, 0)]
        block = jnp.concatenate(blocks, axis=0).T
        return [
            split_parts(block[:, i * side : (i + 1) * side], side, 0) for i in range(len(blocks))
        ]

    def coefficients_x(group_faces):
        courant = turned_parts([coef[0, f] for f in group_faces])
        scaled = turned_parts([coef[1, f] for f in group_faces])
        for f, c, s in zip(group_faces, courant, scaled):
            for k, value in enumerate(stencil(c[0], s[0], c[1], s[1])):
                beta[0, k, f] = value

    def coefficients_y(f):
        c, s = split_parts(coef[0, f], side, 1), split_parts(coef[1, f], side, 1)
        for k, value in enumerate(stencil(c[2], s[2], c[3], s[3])):
            beta[1, k, f] = value

    loop(faces, coefficients_y)
    prod[...] = jnp.zeros_like(prod)
    rim[...] = jnp.zeros_like(rim)
    mirror_id = lax.broadcasted_iota(jnp.int32, (8, 128), 1)
    mirror_id = mirror_id ^ (side - 1)
    upside_id = 7 - lax.broadcasted_iota(jnp.int32, (8, 128), 0)

    def by_lanes(fun, value):
        return jnp.concatenate([fun(value[:, at : at + 128]) for at in range(0, lanes, 128)], axis=1)

    def mirrored(value):
        return by_lanes(lambda chunk: jnp.take_along_axis(chunk, mirror_id, axis=1), value)

    def upside(value):
        return by_lanes(lambda chunk: jnp.take_along_axis(chunk, upside_id, axis=0), value)

    for copy in copies:
        copy.wait()

    def sweep(d, between=None):
        def apply(f):
            cells = field[f]
            here = prod.at[f % slots]
            middle = beta[d, 3, f] * cells
            for k in range(7):
                if k != 3:
                    here[k, PAD : PAD + side, :] = beta[d, k, f] * cells
            before, after = None, None
            for k in (0, 1, 2, 4, 5, 6):
                shift = k - 3
                middle = middle + here[k, PAD - shift : PAD - shift + side, :]
                if shift < 0:
                    term = here[k, PAD - 8 - shift : PAD - shift, :]
                    before = term if before is None else before + term
                else:
                    term = here[k, PAD + side - shift : PAD + side + 8 - shift, :]
                    after = term if after is None else after + term
            acc[f] = middle
            for low, rows in ((0, after), (1, before)):
                orders = (rows, upside(rows))
                for order in range(2):
                    value = orders[order ^ low]
                    rim[0, order, f, low] = value
                    rim[1, order, f, low] = mirrored(value)

        loop(faces, apply)
        if between:
            between()

        def seam(f, edge):
            code = partner_ref[f, edge]
            value = rim[flip_ref[f, edge], int(edge < 2), code >> 2, (code & 3) >> 1]
            return jnp.where((code & 1) == d, value, 0.0)

        def with_seams(value, f, axis):
            return jnp.concatenate(
                [
                    value[0:8] + seam(f, axis + 2),
                    value[8 : side - 8],
                    value[side - 8 :] + seam(f, axis),
                ],
                axis=0,
            )

        def merge(group_faces):
            blocks = turned_parts([with_seams(acc[f], f, d) for f in group_faces])
            for f, parts in zip(group_faces, blocks):
                field[f] = with_seams(jnp.concatenate(parts, axis=1), f, 1 - d)

        over_groups(merge)

    for step in range(STEPS):
        sweep(1, None if step else lambda: over_groups(coefficients_x))
        sweep(0)

    half = 8 // group
    row_id = lax.broadcasted_iota(jnp.int32, (8, slot_lanes), 0) >> (half.bit_length() - 1)
    place = place_id[0:8]

    def tiles_to_rows(block):
        bit = 1
        while bit < group:
            down = pltpu.roll(pltpu.roll(block, 8 - half * bit, 0), bit * cx, 1)
            up = pltpu.roll(pltpu.roll(block, half * bit, 0), slot_lanes - bit * cx, 1)
            a, b = row_id & bit, place & bit
            block = jnp.where(a == b, block, jnp.where(a == 0, down, up))
            bit *= 2
        return block

    count = cy // group

    def hand_out(i):
        f, rows = row_block(i)
        strip = field[f, rows, :]
        for part in range(0, cy, 8):
            block = strip[part : part + 8]
            for first in range(0, tiles_wide, group):
                if group == tiles_wide:
                    value = block
                else:
                    value = jnp.concatenate(
                        [piece[:, first * cx : first * cx + span] for piece in split_parts(block, side, 1)],
                        axis=1,
                    )
                value = tiles_to_rows(value)
                base = (i * tiles_wide + first) * count
                if cy == 8:
                    out_ref[pl.ds(base if isinstance(i, int) else pl.multiple_of(base, 8), 8), :] = value
                else:
                    for a in range(group):
                        out_ref[pl.ds(base + a * count + part // 8 * half, half), :] = value[a * half : (a + 1) * half]

    loop(faces * tiles_high, hand_out)


def in_hbm(array):
    return pltpu.with_memory_space_constraint(array, pltpu.HBM)


def grant(*shapes):
    size = 0
    for *major, rows, columns in shapes:
        size += 4 * math.prod(major) * (-(-rows // 8) * 8) * (-(-columns // 128) * 128)
    return pltpu.CompilerParams(vmem_limit_bytes=size + size // 4 + (2 << 20))


def on_device(cotangent, courant_x, edge_x, courant_y, edge_y, cell_area, seam_partner, seam_flip):
    cells = cotangent[0]
    cy, cx, lanes = cells.shape
    levels = courant_x.shape[-1]
    faces, tiles_high, tiles_wide = (lax.axis_size(axis) for axis in ("face", "ty", "tx"))
    devices = faces * tiles_high * tiles_wide
    side = cx * tiles_wide
    width = PARTS * side
    group = 128 // (PARTS * cx)
    if lanes != PARTS * levels or devices % levels or side != cy * tiles_high:
        raise ValueError("unsupported sizes")
    if cx != 8 or cy % 8 or tiles_wide % group or 128 % side:
        raise ValueError("unsupported tile")
    f32 = jnp.float32
    slot = PARTS * group * cx

    arguments = (
        cells,
        jnp.swapaxes(courant_x[0], 0, 1),
        edge_x[0],
        courant_y[0],
        jnp.swapaxes(edge_y[0], 0, 1),
        cell_area[0],
    )
    pack_rows = (cy * group * cx, lanes)
    send = pl.pallas_call(
        pack_kernel,
        out_shape=jax.ShapeDtypeStruct((levels * cy, slot), f32),
        in_specs=[HBM] * 6,
        out_specs=VMEM,
        scratch_shapes=[
            pltpu.VMEM(pack_rows, f32),
            *[pltpu.VMEM(argument.shape, f32) for argument in arguments[1:]],
            pltpu.SemaphoreType.DMA((5 + cy,)),
        ],
        compiler_params=grant(*[cells.shape] * 4, pack_rows, (levels, cy, slot)),
        name="pack",
    )(*map(in_hbm, arguments))
    if devices > levels:
        send = jnp.tile(send, (devices // levels, 1))
    spheres = lax.all_to_all(send.reshape(devices, cy, slot), AXES, 0, 0, tiled=True)
    scratch = [
        (2, 7, faces, side, width),
        (2, faces, side, width),
        (faces, side, width),
        (faces, side, width),
        (min(faces, 2), 7, side + 2 * PAD, width),
        (2, 2, faces, 2, 8, width),
    ]
    back = (devices * cy // group, slot)
    result = pl.pallas_call(
        functools.partial(sphere_kernel, tiles_high, tiles_wide),
        out_shape=jax.ShapeDtypeStruct(back, f32),
        in_specs=[HBM, HBM, VMEM],
        out_specs=VMEM,
        scratch_shapes=[
            *[pltpu.VMEM(shape, f32) for shape in scratch],
            pltpu.SMEM(seam_partner.shape, jnp.int32),
            pltpu.SMEM(seam_flip.shape, jnp.int32),
            pltpu.SemaphoreType.DMA((2,)),
        ],
        compiler_params=grant((devices, cy, slot), back, *scratch),
        name="sphere",
    )(in_hbm(seam_partner), in_hbm(seam_flip), spheres)
    strips = lax.all_to_all(result, AXES, 0, 0, tiled=True)[: levels * cy // group]
    return pl.pallas_call(
        unpack_kernel,
        out_shape=jax.ShapeDtypeStruct(cells.shape, f32),
        in_specs=[VMEM],
        out_specs=VMEM,
        compiler_params=grant(cells.shape, strips.shape),
        name="unpack",
    )(strips)[None]


def solution(mesh):
    placed = (
        P("face", "ty", "tx", None),
        P("face", "ty", "tx", None),
        P("face", "ty", "tx"),
        P("face", "ty", "tx", None),
        P("face", "ty", "tx"),
        P("face", "ty", "tx"),
        P(),
        P(),
    )
    return jax.shard_map(
        on_device,
        mesh=mesh,
        in_specs=placed,
        out_specs=P("face", "ty", "tx", None),
        check_vma=False,
    )
```

```python
import functools
import math

import jax
import jax.numpy as jnp
from jax import lax
from jax.experimental import pallas as pl
from jax.experimental.pallas import tpu as pltpu
from jax.sharding import PartitionSpec as P

STEPS = 2
AXES = ("ty", "face", "tx")
PARTS = 4
PAD = 16
VMEM = pl.BlockSpec(memory_space=pltpu.VMEM)
HBM = pl.BlockSpec(memory_space=pltpu.HBM)


def loop(count, body):
    if count <= 8:
        for i in range(count):
            body(i)
    else:
        lax.fori_loop(0, count, lambda i, carry: (body(i), carry)[1], 0)


def split_parts(block, width, axis):
    return [lax.slice_in_dim(block, q * width, (q + 1) * width, axis=axis) for q in range(PARTS)]


def turned(block, rows):
    return jnp.concatenate(split_parts(block.T, rows, 0), axis=1)


def pack_kernel(
    cot_hbm, cx_hbm, ex_hbm, cy_hbm, ey_hbm, area_hbm, send_ref, rows_ref, cx_ref, ex_ref, cy_ref, ey_ref, area_ref, sems
):
    cy, cx = area_ref.shape
    lanes = rows_ref.shape[1]
    levels = lanes // PARTS
    group = 128 // (PARTS * cx)
    span = group * cx
    place = [pl.multiple_of(((lax.axis_index("tx") + j) & (group - 1)) * cx, cx) for j in range(3)]
    copies = [
        pltpu.make_async_copy(source, target, sems.at[i])
        for i, (source, target) in enumerate(
            [(ex_hbm, ex_ref), (ey_hbm, ey_ref), (area_hbm, area_ref), (cx_hbm, cx_ref), (cy_hbm, cy_ref)]
            + [(cot_hbm.at[y], rows_ref.at[pl.ds(y * span + place[0], cx)]) for y in range(cy)]
        )
    ]
    for copy in copies:
        copy.start()
    for copy in copies:
        copy.wait()

    for x in range(cx):
        rows_ref[pl.ds(place[1] + x, cy, stride=span), 0 : 2 * levels] = jnp.concatenate(
            [cx_ref[x], cx_ref[x + 1]], axis=1
        )
    for y in range(cy):
        rows_ref[pl.ds(y * span + place[1], cx), 2 * levels :] = jnp.concatenate(
            [cy_ref[y], cy_ref[y + 1]], axis=1
        )

    area = area_ref[...]
    ey = ey_ref[...].T
    gap = jnp.zeros((cy, span - cx), jnp.float32)
    metric = []
    for length in (ex_ref[:, 0:cx], ex_ref[:, 1 : cx + 1], ey[0:cy], ey[1 : cy + 1]):
        metric += [length / area, gap]
    metric = pltpu.roll(jnp.concatenate(metric, axis=1), place[2], 1)
    lane_id = lax.broadcasted_iota(jnp.int32, (levels, lanes), 1)
    here = (lane_id & (span - 1)) >> (cx.bit_length() - 1) == place[2] >> (cx.bit_length() - 1)

    for first in range(0, cy, group):
        block = rows_ref[first * span : (first + group) * span].T
        for i in range(group):
            y = first + i
            row = jnp.concatenate(
                [block[q * levels : (q + 1) * levels, i * span : (i + 1) * span] for q in range(PARTS)],
                axis=1,
            )
            send_ref[pl.ds(y, levels, stride=cy), :] = jnp.where(here, metric[y : y + 1], row)


def unpack_kernel(recv_ref, out_ref):
    cy, cx, lanes = out_ref.shape
    levels = lanes // PARTS
    group = 128 // (PARTS * cx)
    half = 8 // group
    count = cy // group
    for r in range(count):
        block = recv_ref[pl.ds(r, levels, stride=count), :].T
        for b in range(group):
            out_ref[r // half * 8 + b * half + r % half] = jnp.concatenate(
                [block[(q * group + b) * cx : (q * group + b + 1) * cx] for q in range(PARTS)], axis=1
            )


def stencil(*parts):
    c_low, f_low, c_high, f_high = (jnp.concatenate([part] * PARTS, axis=1) for part in parts)

    def interface(c, f):
        size = jnp.abs(c)
        half = 0.5 * size
        w = 3.0 * half * (1.0 - (2.0 / 3.0) * size)
        plus = c > 0
        centre = f * (1.0 - half - w)
        outer = f * (half - w)
        cell = f * (2.0 * w)
        zero = jnp.zeros_like(c)
        o_low, o_high = jnp.where(plus, outer, zero), jnp.where(plus, zero, outer)
        s_low, s_high = jnp.where(plus, cell, zero), jnp.where(plus, zero, cell)
        near, far = 7.0 / 12.0, 1.0 / 12.0
        return (
            -far * o_low,
            near * o_low - far * centre,
            near * (centre + o_low) - far * o_high + s_low,
            near * (centre + o_high) - far * o_low + s_high,
            near * o_high - far * centre,
            -far * o_high,
        )

    low, high = interface(c_low, f_low), interface(c_high, f_high)
    return (
        low[0],
        low[1] - high[0],
        low[2] - high[1],
        1.0 + low[3] - high[2],
        low[4] - high[3],
        low[5] - high[4],
        -high[5],
    )


def sphere_kernel(
    tiles_high,
    tiles_wide,
    partner_hbm,
    flip_hbm,
    recv_ref,
    out_ref,
    beta,
    coef,
    acc,
    field,
    prod,
    rim,
    partner_ref,
    flip_ref,
    sems,
):
    copies = [
        pltpu.make_async_copy(partner_hbm, partner_ref, sems.at[0]),
        pltpu.make_async_copy(flip_hbm, flip_ref, sems.at[1]),
    ]
    for copy in copies:
        copy.start()
    faces, side, lanes = field.shape
    cy, cx = side // tiles_high, side // tiles_wide
    slots = prod.shape[0]
    slot_lanes = recv_ref.shape[2]
    group = slot_lanes // (PARTS * cx)
    span = group * cx
    lane_id = lax.broadcasted_iota(jnp.int32, (cy, slot_lanes), 1)
    place_id = (lane_id >> (cx.bit_length() - 1)) & (group - 1)

    def row_block(i):
        f, ty = i % faces, i // faces
        start = ty * cy
        return f, pl.ds(start if isinstance(i, int) else pl.multiple_of(start, 8), cy)

    def assemble(i):
        f, rows = row_block(i)
        values = []
        for j in range(3):
            blocks = []
            for first in range(0, tiles_wide, group):
                tiles = [recv_ref[i * tiles_wide + first + tx] for tx in range(group)]
                block = tiles[0]
                for tx in range(1, group):
                    block = jnp.where(place_id == (tx + j) % group, tiles[tx], block)
                if j:
                    ahead = pltpu.roll(block, slot_lanes - j * cx, 1)
                    around = pltpu.roll(block, span - j * cx, 1)
                    block = jnp.where(place_id < group - j, ahead, around)
                blocks.append(block)
            if len(blocks) == 1:
                values.append(blocks[0])
            else:
                values.append(
                    jnp.concatenate(
                        [block[:, q * span : (q + 1) * span] for q in range(PARTS) for block in blocks],
                        axis=1,
                    )
                )
        cells, courant, metric = values
        field[f, rows, :] = cells
        coef[0, f, rows, :] = courant
        coef[1, f, rows, :] = courant * metric

    loop(faces * tiles_high, assemble)

    def over_groups(body):
        if faces * side <= 128:
            body(list(range(faces)))
        else:
            loop(faces, lambda f: body([f]))

    def turned_parts(blocks):
        if len(blocks) == 1:
            return [split_parts(blocks[0].T, side, 0)]
        block = jnp.concatenate(blocks, axis=0).T
        return [
            split_parts(block[:, i * side : (i + 1) * side], side, 0) for i in range(len(blocks))
        ]

    def coefficients_x(group_faces):
        courant = turned_parts([coef[0, f] for f in group_faces])
        scaled = turned_parts([coef[1, f] for f in group_faces])
        for f, c, s in zip(group_faces, courant, scaled):
            for k, value in enumerate(stencil(c[0], s[0], c[1], s[1])):
                beta[0, k, f] = value

    def coefficients_y(f):
        c, s = split_parts(coef[0, f], side, 1), split_parts(coef[1, f], side, 1)
        for k, value in enumerate(stencil(c[2], s[2], c[3], s[3])):
            beta[1, k, f] = value

    loop(faces, coefficients_y)
    prod[...] = jnp.zeros_like(prod)
    rim[...] = jnp.zeros_like(rim)
    mirror_id = lax.broadcasted_iota(jnp.int32, (8, 128), 1)
    mirror_id = mirror_id ^ (side - 1)
    upside_id = 7 - lax.broadcasted_iota(jnp.int32, (8, 128), 0)

    def by_lanes(fun, value):
        return jnp.concatenate([fun(value[:, at : at + 128]) for at in range(0, lanes, 128)], axis=1)

    def mirrored(value):
        return by_lanes(lambda chunk: jnp.take_along_axis(chunk, mirror_id, axis=1), value)

    def upside(value):
        return by_lanes(lambda chunk: jnp.take_along_axis(chunk, upside_id, axis=0), value)

    def sweep(d, between=None):
        def apply(f):
            cells = field[f]
            here = prod.at[f % slots]
            middle = beta[d, 3, f] * cells
            for k in range(7):
                if k != 3:
                    here[k, PAD : PAD + side, :] = beta[d, k, f] * cells
            before, after = None, None
            for k in (0, 1, 2, 4, 5, 6):
                shift = k - 3
                middle = middle + here[k, PAD - shift : PAD - shift + side, :]
                if shift < 0:
                    term = here[k, PAD - 8 - shift : PAD - shift, :]
                    before = term if before is None else before + term
                else:
                    term = here[k, PAD + side - shift : PAD + side + 8 - shift, :]
                    after = term if after is None else after + term
            acc[f] = middle
            for low, rows in ((0, after), (1, before)):
                orders = (rows, upside(rows))
                for order in range(2):
                    value = orders[order ^ low]
                    rim[0, order, f, low] = value
                    rim[1, order, f, low] = mirrored(value)

        loop(faces, apply)
        if between:
            between()

        def seam(f, edge):
            code = partner_ref[f, edge]
            value = rim[flip_ref[f, edge], int(edge < 2), code >> 2, (code & 3) >> 1]
            return jnp.where((code & 1) == d, value, 0.0)

        def with_seams(value, f, axis):
            return jnp.concatenate(
                [
                    value[0:8] + seam(f, axis + 2),
                    value[8 : side - 8],
                    value[side - 8 :] + seam(f, axis),
                ],
                axis=0,
            )

        def merge(group_faces):
            blocks = turned_parts([with_seams(acc[f], f, d) for f in group_faces])
            for f, parts in zip(group_faces, blocks):
                field[f] = with_seams(jnp.concatenate(parts, axis=1), f, 1 - d)

        over_groups(merge)

    def between():
        over_groups(coefficients_x)
        for copy in copies:
            copy.wait()

    for step in range(STEPS):
        sweep(1, None if step else between)
        sweep(0)

    half = 8 // group
    row_id = lax.broadcasted_iota(jnp.int32, (8, slot_lanes), 0) >> (half.bit_length() - 1)
    place = place_id[0:8]

    def tiles_to_rows(block):
        bit = 1
        while bit < group:
            down = pltpu.roll(pltpu.roll(block, 8 - half * bit, 0), bit * cx, 1)
            up = pltpu.roll(pltpu.roll(block, half * bit, 0), slot_lanes - bit * cx, 1)
            a, b = row_id & bit, place & bit
            block = jnp.where(a == b, block, jnp.where(a == 0, down, up))
            bit *= 2
        return block

    count = cy // group

    def hand_out(i):
        f, rows = row_block(i)
        strip = field[f, rows, :]
        for part in range(0, cy, 8):
            block = strip[part : part + 8]
            for first in range(0, tiles_wide, group):
                if group == tiles_wide:
                    value = block
                else:
                    value = jnp.concatenate(
                        [piece[:, first * cx : first * cx + span] for piece in split_parts(block, side, 1)],
                        axis=1,
                    )
                value = tiles_to_rows(value)
                base = (i * tiles_wide + first) * count
                if cy == 8:
                    out_ref[pl.ds(base if isinstance(i, int) else pl.multiple_of(base, 8), 8), :] = value
                else:
                    for a in range(group):
                        out_ref[pl.ds(base + a * count + part // 8 * half, half), :] = value[a * half : (a + 1) * half]

    loop(faces * tiles_high, hand_out)


def in_hbm(array):
    return pltpu.with_memory_space_constraint(array, pltpu.HBM)


def grant(*shapes):
    size = 0
    for *major, rows, columns in shapes:
        size += 4 * math.prod(major) * (-(-rows // 8) * 8) * (-(-columns // 128) * 128)
    return pltpu.CompilerParams(vmem_limit_bytes=size + size // 4 + (2 << 20))


def on_device(cotangent, courant_x, edge_x, courant_y, edge_y, cell_area, seam_partner, seam_flip):
    cells = cotangent[0]
    cy, cx, lanes = cells.shape
    levels = courant_x.shape[-1]
    faces, tiles_high, tiles_wide = (lax.axis_size(axis) for axis in ("face", "ty", "tx"))
    devices = faces * tiles_high * tiles_wide
    side = cx * tiles_wide
    width = PARTS * side
    group = 128 // (PARTS * cx)
    if lanes != PARTS * levels or devices % levels or side != cy * tiles_high:
        raise ValueError("unsupported sizes")
    if cx != 8 or cy % 8 or tiles_wide % group or 128 % side:
        raise ValueError("unsupported tile")
    f32 = jnp.float32
    slot = PARTS * group * cx

    arguments = (
        cells,
        jnp.swapaxes(courant_x[0], 0, 1),
        edge_x[0],
        courant_y[0],
        jnp.swapaxes(edge_y[0], 0, 1),
        cell_area[0],
    )
    pack_rows = (cy * group * cx, lanes)
    send = pl.pallas_call(
        pack_kernel,
        out_shape=jax.ShapeDtypeStruct((levels * cy, slot), f32),
        in_specs=[HBM] * 6,
        out_specs=VMEM,
        scratch_shapes=[
            pltpu.VMEM(pack_rows, f32),
            *[pltpu.VMEM(argument.shape, f32) for argument in arguments[1:]],
            pltpu.SemaphoreType.DMA((5 + cy,)),
        ],
        compiler_params=grant(*[cells.shape] * 4, pack_rows, (levels, cy, slot)),
        name="pack",
    )(*map(in_hbm, arguments))
    if devices > levels:
        send = jnp.tile(send, (devices // levels, 1))
    spheres = lax.all_to_all(send.reshape(devices, cy, slot), AXES, 0, 0, tiled=True)
    scratch = [
        (2, 7, faces, side, width),
        (2, faces, side, width),
        (faces, side, width),
        (faces, side, width),
        (min(faces, 2), 7, side + 2 * PAD, width),
        (2, 2, faces, 2, 8, width),
    ]
    back = (devices * cy // group, slot)
    result = pl.pallas_call(
        functools.partial(sphere_kernel, tiles_high, tiles_wide),
        out_shape=jax.ShapeDtypeStruct(back, f32),
        in_specs=[HBM, HBM, VMEM],
        out_specs=VMEM,
        scratch_shapes=[
            *[pltpu.VMEM(shape, f32) for shape in scratch],
            pltpu.SMEM(seam_partner.shape, jnp.int32),
            pltpu.SMEM(seam_flip.shape, jnp.int32),
            pltpu.SemaphoreType.DMA((2,)),
        ],
        compiler_params=grant((devices, cy, slot), back, *scratch),
        name="sphere",
    )(in_hbm(seam_partner), in_hbm(seam_flip), spheres)
    strips = lax.all_to_all(result, AXES, 0, 0, tiled=True)[: levels * cy // group]
    return pl.pallas_call(
        unpack_kernel,
        out_shape=jax.ShapeDtypeStruct(cells.shape, f32),
        in_specs=[VMEM],
        out_specs=VMEM,
        compiler_params=grant(cells.shape, strips.shape),
        name="unpack",
    )(strips)[None]


def solution(mesh):
    placed = (
        P("face", "ty", "tx", None),
        P("face", "ty", "tx", None),
        P("face", "ty", "tx"),
        P("face", "ty", "tx", None),
        P("face", "ty", "tx"),
        P("face", "ty", "tx"),
        P(),
        P(),
    )
    return jax.shard_map(
        on_device,
        mesh=mesh,
        in_specs=placed,
        out_specs=P("face", "ty", "tx", None),
        check_vma=False,
    )
```

```python
import functools
import math

import jax
import jax.numpy as jnp
from jax import lax
from jax.experimental import pallas as pl
from jax.experimental.pallas import tpu as pltpu
from jax.sharding import PartitionSpec as P

STEPS = 2
AXES = ("ty", "face", "tx")
PARTS = 4
PAD = 16
VMEM = pl.BlockSpec(memory_space=pltpu.VMEM)
HBM = pl.BlockSpec(memory_space=pltpu.HBM)


def loop(count, body):
    if count <= 8:
        for i in range(count):
            body(i)
    else:
        lax.fori_loop(0, count, lambda i, carry: (body(i), carry)[1], 0)


def split_parts(block, width, axis):
    return [lax.slice_in_dim(block, q * width, (q + 1) * width, axis=axis) for q in range(PARTS)]


def turned(block, rows):
    return jnp.concatenate(split_parts(block.T, rows, 0), axis=1)


def pack_kernel(
    cot_hbm, cx_hbm, ex_hbm, cy_hbm, ey_hbm, area_hbm, send_ref, rows_ref, cx_ref, ex_ref, cy_ref, ey_ref, area_ref, sems
):
    cy, cx = area_ref.shape
    lanes = rows_ref.shape[1]
    levels = lanes // PARTS
    group = 128 // (PARTS * cx)
    span = group * cx
    count = cy * 3 // 4
    place = [pl.multiple_of(((lax.axis_index("tx") + j) & (group - 1)) * cx, cx) for j in range(4)]

    def home(y, j):
        part, row = y // 8 * 6, y % 8
        if row < 6:
            return (part + row) * span + place[j]
        return (part + (row - 6) * 3 + j) * span + place[3]

    copies = [
        pltpu.make_async_copy(source, target, sems.at[i])
        for i, (source, target) in enumerate(
            [(ex_hbm, ex_ref), (ey_hbm, ey_ref), (area_hbm, area_ref), (cx_hbm, cx_ref), (cy_hbm, cy_ref)]
            + [(cot_hbm.at[y], rows_ref.at[pl.ds(home(y, 0), cx)]) for y in range(cy)]
        )
    ]
    for copy in copies:
        copy.start()
    for copy in copies:
        copy.wait()

    for x in range(cx):
        value = jnp.concatenate([cx_ref[x], cx_ref[x + 1]], axis=1)
        for y in range(0, cy, 8):
            rows_ref[pl.ds(home(y, 1) + x, 6, stride=span), 0 : 2 * levels] = value[y : y + 6]
            rows_ref[pl.ds(home(y + 6, 1) + x, 2, stride=3 * span), 0 : 2 * levels] = value[y + 6 : y + 8]
    for y in range(cy):
        rows_ref[pl.ds(home(y, 1), cx), 2 * levels :] = jnp.concatenate([cy_ref[y], cy_ref[y + 1]], axis=1)

    area = area_ref[...]
    ey = ey_ref[...].T
    gap = jnp.zeros((cy, span - cx), jnp.float32)
    metric = []
    for length in (ex_ref[:, 0:cx], ex_ref[:, 1 : cx + 1], ey[0:cy], ey[1 : cy + 1]):
        metric += [length / area, gap]
    metric = jnp.concatenate(metric, axis=1)
    lane_id = lax.broadcasted_iota(jnp.int32, (levels, lanes), 1)
    first_lane = (lane_id & (span - 1)) & ~(cx - 1)
    metrics = [(first_lane == place[j], pltpu.roll(metric, place[j], 1)) for j in (2, 3)]

    for first in range(0, count, 3):
        block = rows_ref[first * span : (first + 3) * span].T
        for i in range(3):
            r = first + i
            row = jnp.concatenate(
                [block[q * levels : (q + 1) * levels, i * span : (i + 1) * span] for q in range(PARTS)],
                axis=1,
            )
            y = r // 6 * 8 + r % 6
            row = jnp.where(metrics[0][0], metrics[0][1][y : y + 1], row)
            if i == 2:
                y = r // 6 * 8 + 6 + r % 6 // 3
                row = jnp.where(metrics[1][0], metrics[1][1][y : y + 1], row)
            send_ref[pl.ds(r, levels, stride=count), :] = row


def unpack_kernel(recv_ref, out_ref):
    cy, cx, lanes = out_ref.shape
    levels = lanes // PARTS
    group = 128 // (PARTS * cx)
    half = 8 // group
    count = cy // group
    for r in range(count):
        block = recv_ref[pl.ds(r, levels, stride=count), :].T
        for b in range(group):
            out_ref[r // half * 8 + b * half + r % half] = jnp.concatenate(
                [block[(q * group + b) * cx : (q * group + b + 1) * cx] for q in range(PARTS)], axis=1
            )


def stencil(*parts):
    c_low, f_low, c_high, f_high = (jnp.concatenate([part] * PARTS, axis=1) for part in parts)

    def interface(c, f):
        size = jnp.abs(c)
        half = 0.5 * size
        w = 3.0 * half * (1.0 - (2.0 / 3.0) * size)
        plus = c > 0
        centre = f * (1.0 - half - w)
        outer = f * (half - w)
        cell = f * (2.0 * w)
        zero = jnp.zeros_like(c)
        o_low, o_high = jnp.where(plus, outer, zero), jnp.where(plus, zero, outer)
        s_low, s_high = jnp.where(plus, cell, zero), jnp.where(plus, zero, cell)
        near, far = 7.0 / 12.0, 1.0 / 12.0
        return (
            -far * o_low,
            near * o_low - far * centre,
            near * (centre + o_low) - far * o_high + s_low,
            near * (centre + o_high) - far * o_low + s_high,
            near * o_high - far * centre,
            -far * o_high,
        )

    low, high = interface(c_low, f_low), interface(c_high, f_high)
    return (
        low[0],
        low[1] - high[0],
        low[2] - high[1],
        1.0 + low[3] - high[2],
        low[4] - high[3],
        low[5] - high[4],
        -high[5],
    )


def sphere_kernel(
    tiles_high,
    tiles_wide,
    partner_hbm,
    flip_hbm,
    recv_ref,
    out_ref,
    beta,
    coef,
    acc,
    field,
    prod,
    rim,
    partner_ref,
    flip_ref,
    sems,
):
    copies = [
        pltpu.make_async_copy(partner_hbm, partner_ref, sems.at[0]),
        pltpu.make_async_copy(flip_hbm, flip_ref, sems.at[1]),
    ]
    for copy in copies:
        copy.start()
    faces, side, lanes = field.shape
    cy, cx = side // tiles_high, side // tiles_wide
    slots = prod.shape[0]
    slot_lanes = recv_ref.shape[1]
    group = slot_lanes // (PARTS * cx)
    span = group * cx
    lane_id = lax.broadcasted_iota(jnp.int32, (8, slot_lanes), 1)
    place_id = (lane_id >> (cx.bit_length() - 1)) & (group - 1)

    def row_block(i):
        f, ty = i % faces, i // faces
        start = ty * cy
        return f, pl.ds(start if isinstance(i, int) else pl.multiple_of(start, 8), cy)

    count_in = cy * 3 // 4

    def spread(tiles):
        blocks = []
        for j in range(4):
            block = tiles[0]
            for tx in range(1, group):
                block = jnp.where(place_id[0:6] == (tx + j) % group, tiles[tx], block)
            if j:
                ahead = pltpu.roll(block, slot_lanes - j * cx, 1)
                around = pltpu.roll(block, span - j * cx, 1)
                block = jnp.where(place_id[0:6] < group - j, ahead, around)
            blocks.append(block)
        last = blocks[3]
        return [
            jnp.concatenate([blocks[j], last[j : j + 1], last[3 + j : 4 + j]], axis=0) for j in range(3)
        ]

    def assemble(i):
        f, rows = row_block(i)
        for part in range(cy // 8):
            groups = []
            for first in range(0, tiles_wide, group):
                start = (i * tiles_wide + first) * count_in + part * 6
                groups.append(spread([recv_ref[pl.ds(start + tx * count_in, 6), :] for tx in range(group)]))
            values = []
            for blocks in zip(*groups):
                if len(blocks) == 1:
                    values.append(blocks[0])
                    continue
                values.append(
                    jnp.concatenate(
                        [block[:, q * span : (q + 1) * span] for q in range(PARTS) for block in blocks],
                        axis=1,
                    )
                )
            cells, courant, metric = values
            here = pl.ds(i // faces * cy + part * 8, 8)
            if not isinstance(i, int):
                here = pl.ds(pl.multiple_of(i // faces * cy + part * 8, 8), 8)
            field[f, here, :] = cells
            coef[0, f, here, :] = courant
            coef[1, f, here, :] = courant * metric

    loop(faces * tiles_high, assemble)

    def over_groups(body):
        if faces * side <= 128:
            body(list(range(faces)))
        else:
            loop(faces, lambda f: body([f]))

    def turned_parts(blocks):
        if len(blocks) == 1:
            return [split_parts(blocks[0].T, side, 0)]
        block = jnp.concatenate(blocks, axis=0).T
        return [
            split_parts(block[:, i * side : (i + 1) * side], side, 0) for i in range(len(blocks))
        ]

    def coefficients_x(group_faces):
        courant = turned_parts([coef[0, f] for f in group_faces])
        scaled = turned_parts([coef[1, f] for f in group_faces])
        for f, c, s in zip(group_faces, courant, scaled):
            for k, value in enumerate(stencil(c[0], s[0], c[1], s[1])):
                beta[0, k, f] = value

    def coefficients_y(f):
        c, s = split_parts(coef[0, f], side, 1), split_parts(coef[1, f], side, 1)
        for k, value in enumerate(stencil(c[2], s[2], c[3], s[3])):
            beta[1, k, f] = value

    loop(faces, coefficients_y)
    prod[...] = jnp.zeros_like(prod)
    rim[...] = jnp.zeros_like(rim)
    part_id = lax.broadcasted_iota(jnp.int32, (side, lanes), 1) >> (side.bit_length() - 1)
    edge_id = lax.broadcasted_iota(jnp.int32, (8, lanes), 0)
    mirror_id = lax.broadcasted_iota(jnp.int32, (8, 128), 1)
    mirror_id = mirror_id ^ (side - 1)
    upside_id = 7 - lax.broadcasted_iota(jnp.int32, (8, 128), 0)

    def by_lanes(fun, value):
        return jnp.concatenate([fun(value[:, at : at + 128]) for at in range(0, lanes, 128)], axis=1)

    def mirrored(value):
        return by_lanes(lambda chunk: jnp.take_along_axis(chunk, mirror_id, axis=1), value)

    def upside(value):
        return by_lanes(lambda chunk: jnp.take_along_axis(chunk, upside_id, axis=0), value)

    def sweep(d, between=None):
        def overflow(f):
            for low in range(2):
                edge_rows = slice(0, 8) if low else slice(side - 8, side)
                cells = field[f, edge_rows, :]
                rows = None
                for shift in (1, 2, 3):
                    value = beta[d, 3 - shift if low else 3 + shift, f, edge_rows, :] * cells
                    value = pltpu.roll(value, 8 - shift if low else shift, 0)
                    value = jnp.where(edge_id >= 8 - shift if low else edge_id < shift, value, 0.0)
                    rows = value if rows is None else rows + value
                orders = (rows, upside(rows))
                for order in range(2):
                    value = orders[order ^ low]
                    rim[0, order, f, low] = value
                    rim[1, order, f, low] = mirrored(value)

        def apply(f):
            cells = field[f]
            here = prod.at[f % slots]
            middle = beta[d, 3, f] * cells
            for k in range(7):
                if k != 3:
                    here[k, PAD : PAD + side, :] = beta[d, k, f] * cells
            for k in (0, 1, 2, 4, 5, 6):
                middle = middle + here[k, PAD + 3 - k : PAD + 3 - k + side, :]
            acc[f] = middle

        loop(faces, overflow)
        loop(faces, apply)
        if between:
            between()

        def seam(f, edge):
            code = partner_ref[f, edge]
            value = rim[flip_ref[f, edge], int(edge < 2), code >> 2, (code & 3) >> 1]
            return jnp.where((code & 1) == d, value, 0.0)

        def with_seams(value, f, axis):
            return jnp.concatenate(
                [
                    value[0:8] + seam(f, axis + 2),
                    value[8 : side - 8],
                    value[side - 8 :] + seam(f, axis),
                ],
                axis=0,
            )

        def merge(group_faces):
            for f in group_faces:
                block = with_seams(acc[f], f, d)
                if lanes == 128:
                    pieces = split_parts(jnp.concatenate([block] * PARTS, axis=0).T, side, 0)
                    block = pieces[0]
                    for q in range(1, PARTS):
                        block = jnp.where(part_id == q, pieces[q], block)
                else:
                    block = turned(block, side)
                field[f] = with_seams(block, f, 1 - d)

        over_groups(merge)

    def between():
        over_groups(coefficients_x)
        for copy in copies:
            copy.wait()

    for step in range(STEPS):
        sweep(1, None if step else between)
        sweep(0)

    half = 8 // group
    row_id = lax.broadcasted_iota(jnp.int32, (8, slot_lanes), 0) >> (half.bit_length() - 1)
    place = place_id

    def tiles_to_rows(block):
        value = block
        for delta in range(1 - group, group):
            if delta:
                piece = pltpu.roll(block, -half * delta % 8, 0)
                piece = pltpu.roll(piece, delta * cx % slot_lanes, 1)
                value = jnp.where(place - row_id == delta, piece, value)
        return value

    count = cy // group

    def hand_out(i):
        f, rows = row_block(i)
        strip = field[f, rows, :]
        for part in range(0, cy, 8):
            block = strip[part : part + 8]
            for first in range(0, tiles_wide, group):
                if group == tiles_wide:
                    value = block
                else:
                    value = jnp.concatenate(
                        [piece[:, first * cx : first * cx + span] for piece in split_parts(block, side, 1)],
                        axis=1,
                    )
                value = tiles_to_rows(value)
                base = (i * tiles_wide + first) * count
                if cy == 8:
                    out_ref[pl.ds(base if isinstance(i, int) else pl.multiple_of(base, 8), 8), :] = value
                else:
                    for a in range(group):
                        out_ref[pl.ds(base + a * count + part // 8 * half, half), :] = value[a * half : (a + 1) * half]

    loop(faces * tiles_high, hand_out)


def in_hbm(array):
    return pltpu.with_memory_space_constraint(array, pltpu.HBM)


def grant(*shapes):
    size = 0
    for *major, rows, columns in shapes:
        size += 4 * math.prod(major) * (-(-rows // 8) * 8) * (-(-columns // 128) * 128)
    return pltpu.CompilerParams(vmem_limit_bytes=size + size // 4 + (2 << 20))


def on_device(cotangent, courant_x, edge_x, courant_y, edge_y, cell_area, seam_partner, seam_flip):
    cells = cotangent[0]
    cy, cx, lanes = cells.shape
    levels = courant_x.shape[-1]
    faces, tiles_high, tiles_wide = (lax.axis_size(axis) for axis in ("face", "ty", "tx"))
    devices = faces * tiles_high * tiles_wide
    side = cx * tiles_wide
    width = PARTS * side
    group = 128 // (PARTS * cx)
    if lanes != PARTS * levels or devices % levels or side != cy * tiles_high:
        raise ValueError("unsupported sizes")
    if cx != 8 or cy % 8 or tiles_wide % group or 128 % side:
        raise ValueError("unsupported tile")
    f32 = jnp.float32
    slot = PARTS * group * cx

    arguments = (
        cells,
        jnp.swapaxes(courant_x[0], 0, 1),
        edge_x[0],
        courant_y[0],
        jnp.swapaxes(edge_y[0], 0, 1),
        cell_area[0],
    )
    count_in = cy * 3 // 4
    pack_rows = (count_in * group * cx, lanes)
    send = pl.pallas_call(
        pack_kernel,
        out_shape=jax.ShapeDtypeStruct((levels * count_in, slot), f32),
        in_specs=[HBM] * 6,
        out_specs=VMEM,
        scratch_shapes=[
            pltpu.VMEM(pack_rows, f32),
            *[pltpu.VMEM(argument.shape, f32) for argument in arguments[1:]],
            pltpu.SemaphoreType.DMA((5 + cy,)),
        ],
        compiler_params=grant(*[cells.shape] * 4, pack_rows, (levels, cy, slot)),
        name="pack",
    )(*map(in_hbm, arguments))
    if devices > levels:
        send = jnp.tile(send, (devices // levels, 1))
    pairs = send.reshape(devices * count_in // 2, 2, slot)
    spheres = lax.all_to_all(pairs, AXES, 0, 0, tiled=True).reshape(devices * count_in, slot)
    scratch = [
        (2, 7, faces, side, width),
        (2, faces, side, width),
        (faces, side, width),
        (faces, side, width),
        (min(faces, 2), 7, side + 2 * PAD, width),
        (2, 2, faces, 2, 8, width),
    ]
    back = (devices * cy // group, slot)
    result = pl.pallas_call(
        functools.partial(sphere_kernel, tiles_high, tiles_wide),
        out_shape=jax.ShapeDtypeStruct(back, f32),
        in_specs=[HBM, HBM, VMEM],
        out_specs=VMEM,
        scratch_shapes=[
            *[pltpu.VMEM(shape, f32) for shape in scratch],
            pltpu.SMEM(seam_partner.shape, jnp.int32),
            pltpu.SMEM(seam_flip.shape, jnp.int32),
            pltpu.SemaphoreType.DMA((2,)),
        ],
        compiler_params=grant(spheres.shape, back, *scratch),
        name="sphere",
    )(in_hbm(seam_partner), in_hbm(seam_flip), spheres)
    strips = lax.all_to_all(result, AXES, 0, 0, tiled=True)[: levels * cy // group]
    return pl.pallas_call(
        unpack_kernel,
        out_shape=jax.ShapeDtypeStruct(cells.shape, f32),
        in_specs=[VMEM],
        out_specs=VMEM,
        compiler_params=grant(cells.shape, strips.shape),
        name="unpack",
    )(strips)[None]


def solution(mesh):
    placed = (
        P("face", "ty", "tx", None),
        P("face", "ty", "tx", None),
        P("face", "ty", "tx"),
        P("face", "ty", "tx", None),
        P("face", "ty", "tx"),
        P("face", "ty", "tx"),
        P(),
        P(),
    )
    return jax.shard_map(
        on_device,
        mesh=mesh,
        in_specs=placed,
        out_specs=P("face", "ty", "tx", None),
        check_vma=False,
    )
```

```python
import functools
import math

import jax
import jax.numpy as jnp
from jax import lax
from jax.experimental import pallas as pl
from jax.experimental.pallas import tpu as pltpu
from jax.sharding import PartitionSpec as P

STEPS = 2
AXES = ("ty", "face", "tx")
PARTS = 4
PAD = 16
VMEM = pl.BlockSpec(memory_space=pltpu.VMEM)
HBM = pl.BlockSpec(memory_space=pltpu.HBM)


def loop(count, body):
    if count <= 8:
        for i in range(count):
            body(i)
    else:
        lax.fori_loop(0, count, lambda i, carry: (body(i), carry)[1], 0)


def split_parts(block, width, axis):
    return [lax.slice_in_dim(block, q * width, (q + 1) * width, axis=axis) for q in range(PARTS)]


def turned_parts(block, rows):
    if block.shape[0] * PARTS == 128:
        return split_parts(jnp.concatenate([block] * PARTS, axis=0).T, rows, 0)
    return [jnp.concatenate([part] * PARTS, axis=1) for part in split_parts(block.T, rows, 0)]


def joined(parts, part_id):
    value = parts[0]
    for q in range(1, PARTS):
        value = jnp.where(part_id == q, parts[q], value)
    return value


def pack_kernel(
    cot_hbm, cx_hbm, ex_hbm, cy_hbm, ey_hbm, area_hbm, send_ref, rows_ref, cx_ref, ex_ref, cy_ref, ey_ref, area_ref, sems
):
    cy, cx = area_ref.shape
    lanes = rows_ref.shape[1]
    levels = lanes // PARTS
    group = 128 // (PARTS * cx)
    span = group * cx
    count = cy * 3 // 4
    place = [pl.multiple_of(((lax.axis_index("tx") + j) & (group - 1)) * cx, cx) for j in range(4)]

    def home(y, j):
        part, row = y // 8 * 6, y % 8
        if row < 6:
            return (part + row) * span + place[j]
        return (part + (row - 6) * 3 + j) * span + place[3]

    copies = [
        pltpu.make_async_copy(source, target, sems.at[i])
        for i, (source, target) in enumerate(
            [(ex_hbm, ex_ref), (ey_hbm, ey_ref), (area_hbm, area_ref), (cx_hbm, cx_ref), (cy_hbm, cy_ref)]
            + [(cot_hbm.at[y], rows_ref.at[pl.ds(home(y, 0), cx)]) for y in range(cy)]
        )
    ]
    for copy in copies:
        copy.start()
    for copy in copies:
        copy.wait()
    along_x = [jnp.concatenate([cx_ref[x], cx_ref[x + 1]], axis=1) for x in range(cx)]
    along_y = [jnp.concatenate([cy_ref[y], cy_ref[y + 1]], axis=1) for y in range(cy)]
    for x, value in enumerate(along_x):
        for y in range(0, cy, 8):
            rows_ref[pl.ds(home(y, 1) + x, 6, stride=span), 0 : 2 * levels] = value[y : y + 6]
            rows_ref[pl.ds(home(y + 6, 1) + x, 2, stride=3 * span), 0 : 2 * levels] = value[y + 6 : y + 8]
    for y, value in enumerate(along_y):
        rows_ref[pl.ds(home(y, 1), cx), 2 * levels :] = value

    area = area_ref[...]
    ey = ey_ref[...].T
    gap = jnp.zeros((cy, span - cx), jnp.float32)
    metric = []
    for length in (ex_ref[:, 0:cx], ex_ref[:, 1 : cx + 1], ey[0:cy], ey[1 : cy + 1]):
        metric += [length / area, gap]
    metric = jnp.concatenate(metric, axis=1)
    lane_id = lax.broadcasted_iota(jnp.int32, (levels, lanes), 1)
    first_lane = (lane_id & (span - 1)) & ~(cx - 1)
    metrics = [(first_lane == place[j], pltpu.roll(metric, place[j], 1)) for j in (2, 3)]

    part_id = lane_id >> (span.bit_length() - 1)
    for r in range(count):
        row = joined(turned_parts(rows_ref[r * span : (r + 1) * span], levels), part_id)
        y = r // 6 * 8 + r % 6
        row = jnp.where(metrics[0][0], metrics[0][1][y : y + 1], row)
        if r % 3 == 2:
            y = r // 6 * 8 + 6 + r % 6 // 3
            row = jnp.where(metrics[1][0], metrics[1][1][y : y + 1], row)
        send_ref[pl.ds(r, levels, stride=count), :] = row


def unpack_kernel(recv_ref, out_ref):
    cy, cx, lanes = out_ref.shape
    levels = lanes // PARTS
    group = 128 // (PARTS * cx)
    half = 8 // group
    count = cy // group
    part_id = lax.broadcasted_iota(jnp.int32, (cx, lanes), 1) >> (levels.bit_length() - 1)
    for r in range(count):
        pieces = turned_parts(recv_ref[pl.ds(r, levels, stride=count), :], group * cx)
        for b in range(group):
            out_ref[r // half * 8 + b * half + r % half] = joined(
                [piece[b * cx : (b + 1) * cx] for piece in pieces], part_id
            )


def stencil(*parts):
    c_low, f_low, c_high, f_high = parts

    def interface(c, f):
        size = jnp.abs(c)
        half = 0.5 * size
        w = 3.0 * half * (1.0 - (2.0 / 3.0) * size)
        plus = c > 0
        centre = f * (1.0 - half - w)
        outer = f * (half - w)
        cell = f * (2.0 * w)
        zero = jnp.zeros_like(c)
        o_low, o_high = jnp.where(plus, outer, zero), jnp.where(plus, zero, outer)
        s_low, s_high = jnp.where(plus, cell, zero), jnp.where(plus, zero, cell)
        near, far = 7.0 / 12.0, 1.0 / 12.0
        return (
            -far * o_low,
            near * o_low - far * centre,
            near * (centre + o_low) - far * o_high + s_low,
            near * (centre + o_high) - far * o_low + s_high,
            near * o_high - far * centre,
            -far * o_high,
        )

    low, high = interface(c_low, f_low), interface(c_high, f_high)
    return (
        low[0],
        low[1] - high[0],
        low[2] - high[1],
        1.0 + low[3] - high[2],
        low[4] - high[3],
        low[5] - high[4],
        -high[5],
    )


def sphere_kernel(
    tiles_high,
    tiles_wide,
    partner_hbm,
    flip_hbm,
    recv_ref,
    out_ref,
    beta,
    coef,
    acc,
    field,
    prod,
    rim,
    partner_ref,
    flip_ref,
    sems,
):
    copies = [
        pltpu.make_async_copy(partner_hbm, partner_ref, sems.at[0]),
        pltpu.make_async_copy(flip_hbm, flip_ref, sems.at[1]),
    ]
    for copy in copies:
        copy.start()
    faces, side, lanes = field.shape
    cy, cx = side // tiles_high, side // tiles_wide
    slots = prod.shape[0]
    slot_lanes = recv_ref.shape[1]
    group = slot_lanes // (PARTS * cx)
    span = group * cx
    lane_id = lax.broadcasted_iota(jnp.int32, (8, slot_lanes), 1)
    place_id = (lane_id >> (cx.bit_length() - 1)) & (group - 1)

    def row_block(i):
        f, ty = i % faces, i // faces
        start = ty * cy
        return f, pl.ds(start if isinstance(i, int) else pl.multiple_of(start, 8), cy)

    count_in = cy * 3 // 4

    def spread(tiles):
        blocks = []
        for j in range(4):
            block = tiles[0]
            for tx in range(1, group):
                block = jnp.where(place_id[0:6] == (tx + j) % group, tiles[tx], block)
            if j:
                ahead = pltpu.roll(block, slot_lanes - j * cx, 1)
                around = pltpu.roll(block, span - j * cx, 1)
                block = jnp.where(place_id[0:6] < group - j, ahead, around)
            blocks.append(block)
        last = blocks[3]
        return [
            jnp.concatenate([blocks[j], last[j : j + 1], last[3 + j : 4 + j]], axis=0) for j in range(3)
        ]

    def assemble(i):
        f, rows = row_block(i)
        for part in range(cy // 8):
            groups = []
            for first in range(0, tiles_wide, group):
                start = (i * tiles_wide + first) * count_in + part * 6
                groups.append(spread([recv_ref[pl.ds(start + tx * count_in, 6), :] for tx in range(group)]))
            values = []
            for blocks in zip(*groups):
                if len(blocks) == 1:
                    values.append(blocks[0])
                    continue
                values.append(
                    jnp.concatenate(
                        [block[:, q * span : (q + 1) * span] for q in range(PARTS) for block in blocks],
                        axis=1,
                    )
                )
            cells, courant, metric = values
            here = pl.ds(i // faces * cy + part * 8, 8)
            if not isinstance(i, int):
                here = pl.ds(pl.multiple_of(i // faces * cy + part * 8, 8), 8)
            field[f, here, :] = cells
            coef[0, f, here, :] = courant
            coef[1, f, here, :] = courant * metric

    loop(faces * tiles_high, assemble)

    def coefficients_x(f):
        c, s = turned_parts(coef[0, f], side), turned_parts(coef[1, f], side)
        for k, value in enumerate(stencil(c[0], s[0], c[1], s[1])):
            beta[0, k, f] = value

    def coefficients_y(f):
        c, s = (
            [jnp.concatenate([part] * PARTS, axis=1) for part in split_parts(coef[i, f], side, 1)[2:]]
            for i in range(2)
        )
        for k, value in enumerate(stencil(c[0], s[0], c[1], s[1])):
            beta[1, k, f] = value

    loop(faces, coefficients_y)
    prod[...] = jnp.zeros_like(prod)
    rim[...] = jnp.zeros_like(rim)
    part_id = lax.broadcasted_iota(jnp.int32, (side, lanes), 1) >> (side.bit_length() - 1)
    edge_id = lax.broadcasted_iota(jnp.int32, (8, lanes), 0)
    mirror_id = lax.broadcasted_iota(jnp.int32, (8, 128), 1)
    mirror_id = mirror_id ^ (side - 1)
    upside_id = 7 - lax.broadcasted_iota(jnp.int32, (8, 128), 0)

    def by_lanes(fun, value):
        return jnp.concatenate([fun(value[:, at : at + 128]) for at in range(0, lanes, 128)], axis=1)

    def mirrored(value):
        return by_lanes(lambda chunk: jnp.take_along_axis(chunk, mirror_id, axis=1), value)

    def upside(value):
        return by_lanes(lambda chunk: jnp.take_along_axis(chunk, upside_id, axis=0), value)

    def sweep(d, between=None):
        def overflow(f):
            for low in range(2):
                edge_rows = slice(0, 8) if low else slice(side - 8, side)
                cells = field[f, edge_rows, :]
                rows = None
                for shift in (1, 2, 3):
                    value = beta[d, 3 - shift if low else 3 + shift, f, edge_rows, :] * cells
                    value = pltpu.roll(value, 8 - shift if low else shift, 0)
                    value = jnp.where(edge_id >= 8 - shift if low else edge_id < shift, value, 0.0)
                    rows = value if rows is None else rows + value
                orders = (rows, upside(rows))
                for order in range(2):
                    value = orders[order ^ low]
                    rim[0, order, f, low] = value
                    rim[1, order, f, low] = mirrored(value)

        def apply(f):
            cells = field[f]
            here = prod.at[f % slots]
            middle = beta[d, 3, f] * cells
            for k in range(7):
                if k != 3:
                    here[k, PAD : PAD + side, :] = beta[d, k, f] * cells
            for k in (0, 1, 2, 4, 5, 6):
                middle = middle + here[k, PAD + 3 - k : PAD + 3 - k + side, :]
            acc[f] = middle

        loop(faces, overflow)
        loop(faces, apply)
        if between:
            between()

        def seam(f, edge):
            code = partner_ref[f, edge]
            value = rim[flip_ref[f, edge], int(edge < 2), code >> 2, (code & 3) >> 1]
            return jnp.where((code & 1) == d, value, 0.0)

        def with_seams(value, f, axis):
            return jnp.concatenate(
                [
                    value[0:8] + seam(f, axis + 2),
                    value[8 : side - 8],
                    value[side - 8 :] + seam(f, axis),
                ],
                axis=0,
            )

        def merge(f):
            block = joined(turned_parts(with_seams(acc[f], f, d), side), part_id)
            field[f] = with_seams(block, f, 1 - d)

        loop(faces, merge)

    def between():
        loop(faces, coefficients_x)
        for copy in copies:
            copy.wait()

    for step in range(STEPS):
        sweep(1, None if step else between)
        sweep(0)

    half = 8 // group
    row_id = lax.broadcasted_iota(jnp.int32, (8, slot_lanes), 0) >> (half.bit_length() - 1)
    place = place_id

    def tiles_to_rows(block):
        value = block
        for delta in range(1 - group, group):
            if delta:
                piece = pltpu.roll(block, -half * delta % 8, 0)
                piece = pltpu.roll(piece, delta * cx % slot_lanes, 1)
                value = jnp.where(place - row_id == delta, piece, value)
        return value

    count = cy // group

    def hand_out(i):
        f, rows = row_block(i)
        strip = field[f, rows, :]
        for part in range(0, cy, 8):
            block = strip[part : part + 8]
            for first in range(0, tiles_wide, group):
                if group == tiles_wide:
                    value = block
                else:
                    value = jnp.concatenate(
                        [piece[:, first * cx : first * cx + span] for piece in split_parts(block, side, 1)],
                        axis=1,
                    )
                value = tiles_to_rows(value)
                base = (i * tiles_wide + first) * count
                if cy == 8:
                    out_ref[pl.ds(base if isinstance(i, int) else pl.multiple_of(base, 8), 8), :] = value
                else:
                    for a in range(group):
                        out_ref[pl.ds(base + a * count + part // 8 * half, half), :] = value[a * half : (a + 1) * half]

    loop(faces * tiles_high, hand_out)


def in_hbm(array):
    return pltpu.with_memory_space_constraint(array, pltpu.HBM)


def grant(*shapes):
    size = 0
    for *major, rows, columns in shapes:
        size += 4 * math.prod(major) * (-(-rows // 8) * 8) * (-(-columns // 128) * 128)
    return pltpu.CompilerParams(vmem_limit_bytes=size + size // 4 + (2 << 20))


def on_device(cotangent, courant_x, edge_x, courant_y, edge_y, cell_area, seam_partner, seam_flip):
    cells = cotangent[0]
    cy, cx, lanes = cells.shape
    levels = courant_x.shape[-1]
    faces, tiles_high, tiles_wide = (lax.axis_size(axis) for axis in ("face", "ty", "tx"))
    devices = faces * tiles_high * tiles_wide
    side = cx * tiles_wide
    width = PARTS * side
    group = 128 // (PARTS * cx)
    if lanes != PARTS * levels or devices % levels or side != cy * tiles_high:
        raise ValueError("unsupported sizes")
    if cx != 8 or cy % 8 or tiles_wide % group or 128 % side:
        raise ValueError("unsupported tile")
    f32 = jnp.float32
    slot = PARTS * group * cx

    arguments = (
        cells,
        jnp.swapaxes(courant_x[0], 0, 1),
        edge_x[0],
        courant_y[0],
        jnp.swapaxes(edge_y[0], 0, 1),
        cell_area[0],
    )
    count_in = cy * 3 // 4
    pack_rows = (count_in * group * cx, lanes)
    send = pl.pallas_call(
        pack_kernel,
        out_shape=jax.ShapeDtypeStruct((levels * count_in, slot), f32),
        in_specs=[HBM] * 6,
        out_specs=VMEM,
        scratch_shapes=[
            pltpu.VMEM(pack_rows, f32),
            *[pltpu.VMEM(argument.shape, f32) for argument in arguments[1:]],
            pltpu.SemaphoreType.DMA((5 + cy,)),
        ],
        compiler_params=grant(*[cells.shape] * 4, pack_rows, (levels, cy, slot)),
        name="pack",
    )(*map(in_hbm, arguments))
    if devices > levels:
        send = jnp.tile(send, (devices // levels, 1))
    pairs = send.reshape(devices * count_in // 2, 2, slot)
    spheres = lax.all_to_all(pairs, AXES, 0, 0, tiled=True).reshape(devices * count_in, slot)
    scratch = [
        (2, 7, faces, side, width),
        (2, faces, side, width),
        (faces, side, width),
        (faces, side, width),
        (min(faces, 2), 7, side + 2 * PAD, width),
        (2, 2, faces, 2, 8, width),
    ]
    back = (devices * cy // group, slot)
    result = pl.pallas_call(
        functools.partial(sphere_kernel, tiles_high, tiles_wide),
        out_shape=jax.ShapeDtypeStruct(back, f32),
        in_specs=[HBM, HBM, VMEM],
        out_specs=VMEM,
        scratch_shapes=[
            *[pltpu.VMEM(shape, f32) for shape in scratch],
            pltpu.SMEM(seam_partner.shape, jnp.int32),
            pltpu.SMEM(seam_flip.shape, jnp.int32),
            pltpu.SemaphoreType.DMA((2,)),
        ],
        compiler_params=grant(spheres.shape, back, *scratch),
        name="sphere",
    )(in_hbm(seam_partner), in_hbm(seam_flip), spheres)
    strips = lax.all_to_all(result, AXES, 0, 0, tiled=True)[: levels * cy // group]
    return pl.pallas_call(
        unpack_kernel,
        out_shape=jax.ShapeDtypeStruct(cells.shape, f32),
        in_specs=[VMEM],
        out_specs=VMEM,
        compiler_params=grant(cells.shape, strips.shape),
        name="unpack",
    )(strips)[None]


def solution(mesh):
    placed = (
        P("face", "ty", "tx", None),
        P("face", "ty", "tx", None),
        P("face", "ty", "tx"),
        P("face", "ty", "tx", None),
        P("face", "ty", "tx"),
        P("face", "ty", "tx"),
        P(),
        P(),
    )
    return jax.shard_map(
        on_device,
        mesh=mesh,
        in_specs=placed,
        out_specs=P("face", "ty", "tx", None),
        check_vma=False,
    )
```

```python
import functools
import math

import jax
import jax.numpy as jnp
from jax import lax
from jax.experimental import pallas as pl
from jax.experimental.pallas import tpu as pltpu
from jax.sharding import PartitionSpec as P

STEPS = 2
AXES = ("ty", "face", "tx")
PARTS = 4
PAD = 16
VMEM = pl.BlockSpec(memory_space=pltpu.VMEM)
HBM = pl.BlockSpec(memory_space=pltpu.HBM)


def loop(count, body):
    if count <= 8:
        for i in range(count):
            body(i)
    else:
        lax.fori_loop(0, count, lambda i, carry: (body(i), carry)[1], 0)


def split_parts(block, width, axis):
    return [lax.slice_in_dim(block, q * width, (q + 1) * width, axis=axis) for q in range(PARTS)]


def turned_parts(block, rows):
    if block.shape[0] * PARTS == 128:
        return split_parts(jnp.concatenate([block] * PARTS, axis=0).T, rows, 0)
    return [jnp.concatenate([part] * PARTS, axis=1) for part in split_parts(block.T, rows, 0)]


def joined(parts, part_id):
    value = parts[0]
    for q in range(1, PARTS):
        value = jnp.where(part_id == q, parts[q], value)
    return value


def pack_kernel(
    cot_hbm,
    cx_hbm,
    ex_hbm,
    cy_hbm,
    ey_hbm,
    area_hbm,
    partner_hbm,
    flip_hbm,
    send_ref,
    partner_ref,
    flip_ref,
    rows_ref,
    cx_ref,
    ex_ref,
    cy_ref,
    ey_ref,
    area_ref,
    sems,
):
    cy, cx = area_ref.shape
    lanes = rows_ref.shape[1]
    levels = lanes // PARTS
    group = 128 // (PARTS * cx)
    span = group * cx
    count = cy * 3 // 4
    place = [pl.multiple_of(((lax.axis_index("tx") + j) & (group - 1)) * cx, cx) for j in range(4)]

    def home(y, j):
        part, row = y // 8 * 6, y % 8
        if row < 6:
            return (part + row) * span + place[j]
        return (part + (row - 6) * 3 + j) * span + place[3]

    copies = [
        pltpu.make_async_copy(source, target, sems.at[i])
        for i, (source, target) in enumerate(
            [(ex_hbm, ex_ref), (ey_hbm, ey_ref), (area_hbm, area_ref), (cx_hbm, cx_ref), (cy_hbm, cy_ref)]
            + [(cot_hbm.at[y], rows_ref.at[pl.ds(home(y, 0), cx)]) for y in range(cy)]
            + [(partner_hbm, partner_ref), (flip_hbm, flip_ref)]
        )
    ]
    for copy in copies:
        copy.start()
    for copy in copies[:-2]:
        copy.wait()
    along_x = [jnp.concatenate([cx_ref[x], cx_ref[x + 1]], axis=1) for x in range(cx)]
    along_y = [jnp.concatenate([cy_ref[y], cy_ref[y + 1]], axis=1) for y in range(cy)]
    for x, value in enumerate(along_x):
        for y in range(0, cy, 8):
            rows_ref[pl.ds(home(y, 1) + x, 6, stride=span), 0 : 2 * levels] = value[y : y + 6]
            rows_ref[pl.ds(home(y + 6, 1) + x, 2, stride=3 * span), 0 : 2 * levels] = value[y + 6 : y + 8]
    for y, value in enumerate(along_y):
        rows_ref[pl.ds(home(y, 1), cx), 2 * levels :] = value

    area = 12.0 * area_ref[...]
    ey = ey_ref[...].T
    gap = jnp.zeros((cy, span - cx), jnp.float32)
    metric = []
    for length in (ex_ref[:, 0:cx], ex_ref[:, 1 : cx + 1], ey[0:cy], ey[1 : cy + 1]):
        metric += [length / area, gap]
    metric = jnp.concatenate(metric, axis=1)
    lane_id = lax.broadcasted_iota(jnp.int32, (levels, lanes), 1)
    first_lane = (lane_id & (span - 1)) & ~(cx - 1)
    metrics = [(first_lane == place[j], pltpu.roll(metric, place[j], 1)) for j in (2, 3)]

    part_id = lane_id >> (span.bit_length() - 1)
    for r in range(count):
        row = joined(turned_parts(rows_ref[r * span : (r + 1) * span], levels), part_id)
        y = r // 6 * 8 + r % 6
        row = jnp.where(metrics[0][0], metrics[0][1][y : y + 1], row)
        if r % 3 == 2:
            y = r // 6 * 8 + 6 + r % 6 // 3
            row = jnp.where(metrics[1][0], metrics[1][1][y : y + 1], row)
        send_ref[pl.ds(r, levels, stride=count), :] = row
    for copy in copies[-2:]:
        copy.wait()


def unpack_kernel(recv_ref, out_ref):
    cy, cx, lanes = out_ref.shape
    levels = lanes // PARTS
    group = 128 // (PARTS * cx)
    half = 8 // group
    count = cy // group
    part_id = lax.broadcasted_iota(jnp.int32, (cx, lanes), 1) >> (levels.bit_length() - 1)
    for r in range(count):
        pieces = turned_parts(recv_ref[pl.ds(r, levels, stride=count), :], group * cx)
        for b in range(group):
            out_ref[r // half * 8 + b * half + r % half] = joined(
                [piece[b * cx : (b + 1) * cx] for piece in pieces], part_id
            )


def stencil(*parts):
    c_low, f_low, c_high, f_high = parts

    def interface(c, f):
        size = jnp.abs(c)
        rest = 1.0 - size
        part = f * size
        centre = f * rest * rest
        outer = part * rest
        cell = part * (12.0 + 24.0 * rest)
        middle = 7.0 * centre
        cell = cell - 7.0 * outer
        plus = c > 0
        first = jnp.where(plus, outer, 0.0)
        last = outer - first
        return (
            first,
            -7.0 * first - centre,
            middle + jnp.where(plus, cell, outer),
            middle + jnp.where(plus, outer, cell),
            -7.0 * last - centre,
            last,
        )

    low, high = interface(c_low, f_low), interface(c_high, f_high)
    return (
        low[0],
        low[1] - high[0],
        low[2] - high[1],
        1.0 + low[3] - high[2],
        low[4] - high[3],
        low[5] - high[4],
        -high[5],
    )


def sphere_kernel(
    tiles_high,
    tiles_wide,
    partner_vmem,
    flip_vmem,
    recv_ref,
    out_ref,
    beta,
    coef,
    acc,
    field,
    prod,
    rim,
    partner_ref,
    flip_ref,
    sems,
):
    copies = [
        pltpu.make_async_copy(partner_vmem, partner_ref, sems.at[0]),
        pltpu.make_async_copy(flip_vmem, flip_ref, sems.at[1]),
    ]
    for copy in copies:
        copy.start()
    faces, side, lanes = field.shape
    cy, cx = side // tiles_high, side // tiles_wide
    slots = prod.shape[0]
    slot_lanes = recv_ref.shape[1]
    group = slot_lanes // (PARTS * cx)
    span = group * cx
    lane_id = lax.broadcasted_iota(jnp.int32, (8, slot_lanes), 1)
    place_id = (lane_id >> (cx.bit_length() - 1)) & (group - 1)

    def row_block(i):
        f, ty = i % faces, i // faces
        start = ty * cy
        return f, pl.ds(start if isinstance(i, int) else pl.multiple_of(start, 8), cy)

    count_in = cy * 3 // 4

    def spread(tiles):
        blocks = []
        for j in range(4):
            block = tiles[0]
            for tx in range(1, group):
                block = jnp.where(place_id[0:6] == (tx + j) % group, tiles[tx], block)
            if j:
                ahead = pltpu.roll(block, slot_lanes - j * cx, 1)
                around = pltpu.roll(block, span - j * cx, 1)
                block = jnp.where(place_id[0:6] < group - j, ahead, around)
            blocks.append(block)
        last = blocks[3]
        return [
            jnp.concatenate([blocks[j], last[j : j + 1], last[3 + j : 4 + j]], axis=0) for j in range(3)
        ]

    def assemble(i):
        f, rows = row_block(i)
        for part in range(cy // 8):
            groups = []
            for first in range(0, tiles_wide, group):
                start = (i * tiles_wide + first) * count_in + part * 6
                groups.append(spread([recv_ref[pl.ds(start + tx * count_in, 6), :] for tx in range(group)]))
            values = []
            for blocks in zip(*groups):
                if len(blocks) == 1:
                    values.append(blocks[0])
                    continue
                values.append(
                    jnp.concatenate(
                        [block[:, q * span : (q + 1) * span] for q in range(PARTS) for block in blocks],
                        axis=1,
                    )
                )
            cells, courant, metric = values
            here = pl.ds(i // faces * cy + part * 8, 8)
            if not isinstance(i, int):
                here = pl.ds(pl.multiple_of(i // faces * cy + part * 8, 8), 8)
            field[f, here, :] = cells
            coef[0, f, here, :] = courant
            coef[1, f, here, :] = courant * metric

    loop(faces * tiles_high, assemble)

    def coefficients_x(f):
        c, s = turned_parts(coef[0, f], side), turned_parts(coef[1, f], side)
        for k, value in enumerate(stencil(c[0], s[0], c[1], s[1])):
            beta[0, k, f] = value

    def coefficients_y(f):
        c, s = (
            [jnp.concatenate([part] * PARTS, axis=1) for part in split_parts(coef[i, f], side, 1)[2:]]
            for i in range(2)
        )
        for k, value in enumerate(stencil(c[0], s[0], c[1], s[1])):
            beta[1, k, f] = value

    loop(faces, coefficients_y)
    prod[...] = jnp.zeros_like(prod)
    rim[...] = jnp.zeros_like(rim)
    part_id = lax.broadcasted_iota(jnp.int32, (side, lanes), 1) >> (side.bit_length() - 1)
    edge_id = lax.broadcasted_iota(jnp.int32, (8, lanes), 0)
    mirror_id = lax.broadcasted_iota(jnp.int32, (8, 128), 1)
    mirror_id = mirror_id ^ (side - 1)
    upside_id = 7 - lax.broadcasted_iota(jnp.int32, (8, 128), 0)

    def by_lanes(fun, value):
        return jnp.concatenate([fun(value[:, at : at + 128]) for at in range(0, lanes, 128)], axis=1)

    def mirrored(value):
        return by_lanes(lambda chunk: jnp.take_along_axis(chunk, mirror_id, axis=1), value)

    def upside(value):
        return by_lanes(lambda chunk: jnp.take_along_axis(chunk, upside_id, axis=0), value)

    def sweep(d, between=None):
        def overflow(f):
            for low in range(2):
                edge_rows = slice(0, 8) if low else slice(side - 8, side)
                cells = field[f, edge_rows, :]
                rows = None
                for shift in (1, 2, 3):
                    value = beta[d, 3 - shift if low else 3 + shift, f, edge_rows, :] * cells
                    value = pltpu.roll(value, 8 - shift if low else shift, 0)
                    value = jnp.where(edge_id >= 8 - shift if low else edge_id < shift, value, 0.0)
                    rows = value if rows is None else rows + value
                orders = (rows, upside(rows))
                for order in range(2):
                    value = orders[order ^ low]
                    rim[0, order, f, low] = value
                    rim[1, order, f, low] = mirrored(value)

        def apply(f):
            cells = field[f]
            here = prod.at[f % slots]
            middle = beta[d, 3, f] * cells
            for k in range(7):
                if k != 3:
                    here[k, PAD : PAD + side, :] = beta[d, k, f] * cells
            for k in (0, 1, 2, 4, 5, 6):
                middle = middle + here[k, PAD + 3 - k : PAD + 3 - k + side, :]
            acc[f] = middle

        loop(faces, overflow)
        loop(faces, apply)
        if between:
            between()

        def seam(f, edge):
            code = partner_ref[f, edge]
            value = rim[flip_ref[f, edge], int(edge < 2), code >> 2, (code & 3) >> 1]
            return jnp.where((code & 1) == d, value, 0.0)

        def with_seams(value, f, axis):
            return jnp.concatenate(
                [
                    value[0:8] + seam(f, axis + 2),
                    value[8 : side - 8],
                    value[side - 8 :] + seam(f, axis),
                ],
                axis=0,
            )

        def merge(f):
            block = joined(turned_parts(with_seams(acc[f], f, d), side), part_id)
            field[f] = with_seams(block, f, 1 - d)

        loop(faces, merge)

    def between():
        loop(faces, coefficients_x)
        for copy in copies:
            copy.wait()

    for step in range(STEPS):
        sweep(1, None if step else between)
        sweep(0)

    half = 8 // group
    row_id = lax.broadcasted_iota(jnp.int32, (8, slot_lanes), 0) >> (half.bit_length() - 1)
    place = place_id

    def tiles_to_rows(block):
        value = block
        for delta in range(1 - group, group):
            if delta:
                piece = pltpu.roll(block, -half * delta % 8, 0)
                piece = pltpu.roll(piece, delta * cx % slot_lanes, 1)
                value = jnp.where(place - row_id == delta, piece, value)
        return value

    count = cy // group

    def hand_out(i):
        f, rows = row_block(i)
        strip = field[f, rows, :]
        for part in range(0, cy, 8):
            block = strip[part : part + 8]
            for first in range(0, tiles_wide, group):
                if group == tiles_wide:
                    value = block
                else:
                    value = jnp.concatenate(
                        [piece[:, first * cx : first * cx + span] for piece in split_parts(block, side, 1)],
                        axis=1,
                    )
                value = tiles_to_rows(value)
                base = (i * tiles_wide + first) * count
                if cy == 8:
                    out_ref[pl.ds(base if isinstance(i, int) else pl.multiple_of(base, 8), 8), :] = value
                else:
                    for a in range(group):
                        out_ref[pl.ds(base + a * count + part // 8 * half, half), :] = value[a * half : (a + 1) * half]

    loop(faces * tiles_high, hand_out)


def in_hbm(array):
    return pltpu.with_memory_space_constraint(array, pltpu.HBM)


def grant(*shapes):
    size = 0
    for *major, rows, columns in shapes:
        size += 4 * math.prod(major) * (-(-rows // 8) * 8) * (-(-columns // 128) * 128)
    return pltpu.CompilerParams(vmem_limit_bytes=size + size // 4 + (2 << 20))


def on_device(cotangent, courant_x, edge_x, courant_y, edge_y, cell_area, seam_partner, seam_flip):
    cells = cotangent[0]
    cy, cx, lanes = cells.shape
    levels = courant_x.shape[-1]
    faces, tiles_high, tiles_wide = (lax.axis_size(axis) for axis in ("face", "ty", "tx"))
    devices = faces * tiles_high * tiles_wide
    side = cx * tiles_wide
    width = PARTS * side
    group = 128 // (PARTS * cx)
    if lanes != PARTS * levels or devices % levels or side != cy * tiles_high:
        raise ValueError("unsupported sizes")
    if cx != 8 or cy % 8 or tiles_wide % group or 128 % side:
        raise ValueError("unsupported tile")
    f32 = jnp.float32
    slot = PARTS * group * cx

    arguments = (
        cells,
        jnp.swapaxes(courant_x[0], 0, 1),
        edge_x[0],
        courant_y[0],
        jnp.swapaxes(edge_y[0], 0, 1),
        cell_area[0],
        seam_partner,
        seam_flip,
    )
    count_in = cy * 3 // 4
    pack_rows = (count_in * group * cx, lanes)
    send, partner, flip = pl.pallas_call(
        pack_kernel,
        out_shape=(
            jax.ShapeDtypeStruct((levels * count_in, slot), f32),
            jax.ShapeDtypeStruct(seam_partner.shape, jnp.int32),
            jax.ShapeDtypeStruct(seam_flip.shape, jnp.int32),
        ),
        in_specs=[HBM] * 8,
        out_specs=(VMEM, VMEM, VMEM),
        scratch_shapes=[
            pltpu.VMEM(pack_rows, f32),
            *[pltpu.VMEM(argument.shape, f32) for argument in arguments[1:6]],
            pltpu.SemaphoreType.DMA((7 + cy,)),
        ],
        compiler_params=grant(*[cells.shape] * 4, pack_rows, (levels, cy, slot)),
        name="pack",
    )(*map(in_hbm, arguments))
    if devices > levels:
        send = jnp.tile(send, (devices // levels, 1))
    pairs = send.reshape(devices * count_in // 2, 2, slot)
    spheres = lax.all_to_all(pairs, AXES, 0, 0, tiled=True).reshape(devices * count_in, slot)
    scratch = [
        (2, 7, faces, side, width),
        (2, faces, side, width),
        (faces, side, width),
        (faces, side, width),
        (min(faces, 2), 7, side + 2 * PAD, width),
        (2, 2, faces, 2, 8, width),
    ]
    back = (devices * cy // group, slot)
    result = pl.pallas_call(
        functools.partial(sphere_kernel, tiles_high, tiles_wide),
        out_shape=jax.ShapeDtypeStruct(back, f32),
        in_specs=[VMEM, VMEM, VMEM],
        out_specs=VMEM,
        scratch_shapes=[
            *[pltpu.VMEM(shape, f32) for shape in scratch],
            pltpu.SMEM(seam_partner.shape, jnp.int32),
            pltpu.SMEM(seam_flip.shape, jnp.int32),
            pltpu.SemaphoreType.DMA((2,)),
        ],
        compiler_params=grant(spheres.shape, back, *scratch),
        name="sphere",
    )(partner, flip, spheres)
    strips = lax.all_to_all(result, AXES, 0, 0, tiled=True)[: levels * cy // group]
    return pl.pallas_call(
        unpack_kernel,
        out_shape=jax.ShapeDtypeStruct(cells.shape, f32),
        in_specs=[VMEM],
        out_specs=VMEM,
        compiler_params=grant(cells.shape, strips.shape),
        name="unpack",
    )(strips)[None]


def solution(mesh):
    placed = (
        P("face", "ty", "tx", None),
        P("face", "ty", "tx", None),
        P("face", "ty", "tx"),
        P("face", "ty", "tx", None),
        P("face", "ty", "tx"),
        P("face", "ty", "tx"),
        P(),
        P(),
    )
    return jax.shard_map(
        on_device,
        mesh=mesh,
        in_specs=placed,
        out_specs=P("face", "ty", "tx", None),
        check_vma=False,
    )
```

```python
import functools
import math

import jax
import jax.numpy as jnp
from jax import lax
from jax.experimental import pallas as pl
from jax.experimental.pallas import tpu as pltpu
from jax.sharding import PartitionSpec as P

STEPS = 2
AXES = ("ty", "face", "tx")
PARTS = 4
PAD = 16
VMEM = pl.BlockSpec(memory_space=pltpu.VMEM)
HBM = pl.BlockSpec(memory_space=pltpu.HBM)


def loop(count, body):
    if count <= 8:
        for i in range(count):
            body(i)
    else:
        lax.fori_loop(0, count, lambda i, carry: (body(i), carry)[1], 0)


def split_parts(block, width, axis):
    return [lax.slice_in_dim(block, q * width, (q + 1) * width, axis=axis) for q in range(PARTS)]


def turned_parts(block, rows):
    if block.shape[0] * PARTS == 128:
        return split_parts(jnp.concatenate([block] * PARTS, axis=0).T, rows, 0)
    return [jnp.concatenate([part] * PARTS, axis=1) for part in split_parts(block.T, rows, 0)]


def joined(parts, part_id):
    value = parts[0]
    for q in range(1, PARTS):
        value = jnp.where(part_id == q, parts[q], value)
    return value


def pack_kernel(
    cot_hbm,
    cx_hbm,
    ex_hbm,
    cy_hbm,
    ey_hbm,
    area_hbm,
    partner_hbm,
    flip_hbm,
    send_ref,
    partner_ref,
    flip_ref,
    rows_ref,
    cot_ref,
    cx_ref,
    ex_ref,
    cy_ref,
    ey_ref,
    area_ref,
    sems,
):
    cy, cx = area_ref.shape
    lanes = rows_ref.shape[1]
    levels = lanes // PARTS
    group = 128 // (PARTS * cx)
    span = group * cx
    count = cy * 3 // 4
    place = [pl.multiple_of(((lax.axis_index("tx") + j) & (group - 1)) * cx, cx) for j in range(4)]

    def home(y, j):
        part, row = y // 8 * 6, y % 8
        if row < 6:
            return (part + row) * span + place[j]
        return (part + (row - 6) * 3 + j) * span + place[3]

    copies = [
        pltpu.make_async_copy(source, target, sems.at[i])
        for i, (source, target) in enumerate(
            [(cx_hbm, cx_ref), (cy_hbm, cy_ref), (cot_hbm, cot_ref), (ex_hbm, ex_ref), (ey_hbm, ey_ref)]
            + [(area_hbm, area_ref)]
            + [(partner_hbm, partner_ref), (flip_hbm, flip_ref)]
        )
    ]
    for copy in copies:
        copy.start()
    for copy in copies[:-2]:
        copy.wait()
    for y in range(cy):
        rows_ref[pl.ds(home(y, 0), cx), :] = cot_ref[y]
    along_x = [jnp.concatenate([cx_ref[x], cx_ref[x + 1]], axis=1) for x in range(cx)]
    along_y = [jnp.concatenate([cy_ref[y], cy_ref[y + 1]], axis=1) for y in range(cy)]
    for x, value in enumerate(along_x):
        for y in range(0, cy, 8):
            rows_ref[pl.ds(home(y, 1) + x, 6, stride=span), 0 : 2 * levels] = value[y : y + 6]
            rows_ref[pl.ds(home(y + 6, 1) + x, 2, stride=3 * span), 0 : 2 * levels] = value[y + 6 : y + 8]
    for y, value in enumerate(along_y):
        rows_ref[pl.ds(home(y, 1), cx), 2 * levels :] = value

    area = 12.0 * area_ref[...]
    ey = ey_ref[...].T
    gap = jnp.zeros((cy, span - cx), jnp.float32)
    metric = []
    for length in (ex_ref[:, 0:cx], ex_ref[:, 1 : cx + 1], ey[0:cy], ey[1 : cy + 1]):
        metric += [length / area, gap]
    metric = jnp.concatenate(metric, axis=1)
    lane_id = lax.broadcasted_iota(jnp.int32, (levels, lanes), 1)
    first_lane = (lane_id & (span - 1)) & ~(cx - 1)
    metrics = [(first_lane == place[j], pltpu.roll(metric, place[j], 1)) for j in (2, 3)]

    part_id = lane_id >> (span.bit_length() - 1)
    for r in range(count):
        row = joined(turned_parts(rows_ref[r * span : (r + 1) * span], levels), part_id)
        y = r // 6 * 8 + r % 6
        row = jnp.where(metrics[0][0], metrics[0][1][y : y + 1], row)
        if r % 3 == 2:
            y = r // 6 * 8 + 6 + r % 6 // 3
            row = jnp.where(metrics[1][0], metrics[1][1][y : y + 1], row)
        send_ref[pl.ds(r, levels, stride=count), :] = row
    for copy in copies[-2:]:
        copy.wait()


def unpack_kernel(recv_ref, out_ref):
    cy, cx, lanes = out_ref.shape
    levels = lanes // PARTS
    group = 128 // (PARTS * cx)
    half = 8 // group
    count = cy // group
    part_id = lax.broadcasted_iota(jnp.int32, (cx, lanes), 1) >> (levels.bit_length() - 1)
    for r in range(count):
        pieces = turned_parts(recv_ref[pl.ds(r, levels, stride=count), :], group * cx)
        for b in range(group):
            out_ref[r // half * 8 + b * half + r % half] = joined(
                [piece[b * cx : (b + 1) * cx] for piece in pieces], part_id
            )


def stencil(*parts):
    c_low, f_low, c_high, f_high = parts

    def interface(c, f):
        size = jnp.abs(c)
        rest = 1.0 - size
        part = f * size
        centre = f * rest * rest
        outer = part * rest
        cell = part * (12.0 + 24.0 * rest)
        middle = 7.0 * centre
        cell = cell - 7.0 * outer
        plus = c > 0
        first = jnp.where(plus, outer, 0.0)
        last = outer - first
        return (
            first,
            -7.0 * first - centre,
            middle + jnp.where(plus, cell, outer),
            middle + jnp.where(plus, outer, cell),
            -7.0 * last - centre,
            last,
        )

    low, high = interface(c_low, f_low), interface(c_high, f_high)
    return (
        low[0],
        low[1] - high[0],
        low[2] - high[1],
        1.0 + low[3] - high[2],
        low[4] - high[3],
        low[5] - high[4],
        -high[5],
    )


def sphere_kernel(
    tiles_high,
    tiles_wide,
    partner_vmem,
    flip_vmem,
    recv_ref,
    out_ref,
    beta,
    coef,
    acc,
    field,
    prod,
    rim,
    partner_ref,
    flip_ref,
    sems,
):
    copies = [
        pltpu.make_async_copy(partner_vmem, partner_ref, sems.at[0]),
        pltpu.make_async_copy(flip_vmem, flip_ref, sems.at[1]),
    ]
    for copy in copies:
        copy.start()
    faces, side, lanes = field.shape
    cy, cx = side // tiles_high, side // tiles_wide
    slots = prod.shape[0]
    slot_lanes = recv_ref.shape[1]
    group = slot_lanes // (PARTS * cx)
    span = group * cx
    lane_id = lax.broadcasted_iota(jnp.int32, (8, slot_lanes), 1)
    place_id = (lane_id >> (cx.bit_length() - 1)) & (group - 1)

    def row_block(i):
        f, ty = i % faces, i // faces
        start = ty * cy
        return f, pl.ds(start if isinstance(i, int) else pl.multiple_of(start, 8), cy)

    count_in = cy * 3 // 4

    def spread(tiles):
        blocks = []
        for j in range(4):
            block = tiles[0]
            for tx in range(1, group):
                block = jnp.where(place_id[0:6] == (tx + j) % group, tiles[tx], block)
            if j:
                ahead = pltpu.roll(block, slot_lanes - j * cx, 1)
                around = pltpu.roll(block, span - j * cx, 1)
                block = jnp.where(place_id[0:6] < group - j, ahead, around)
            blocks.append(block)
        last = blocks[3]
        return [
            jnp.concatenate([blocks[j], last[j : j + 1], last[3 + j : 4 + j]], axis=0) for j in range(3)
        ]

    def assemble(i):
        f, rows = row_block(i)
        for part in range(cy // 8):
            groups = []
            for first in range(0, tiles_wide, group):
                start = (i * tiles_wide + first) * count_in + part * 6
                groups.append(spread([recv_ref[pl.ds(start + tx * count_in, 6), :] for tx in range(group)]))
            values = []
            for blocks in zip(*groups):
                if len(blocks) == 1:
                    values.append(blocks[0])
                    continue
                values.append(
                    jnp.concatenate(
                        [block[:, q * span : (q + 1) * span] for q in range(PARTS) for block in blocks],
                        axis=1,
                    )
                )
            cells, courant, metric = values
            here = pl.ds(i // faces * cy + part * 8, 8)
            if not isinstance(i, int):
                here = pl.ds(pl.multiple_of(i // faces * cy + part * 8, 8), 8)
            field[f, here, :] = cells
            coef[0, f, here, :] = courant
            coef[1, f, here, :] = courant * metric

    loop(faces * tiles_high, assemble)

    def coefficients_x(f):
        c, s = turned_parts(coef[0, f], side), turned_parts(coef[1, f], side)
        for k, value in enumerate(stencil(c[0], s[0], c[1], s[1])):
            beta[0, k, f] = value

    def coefficients_y(f):
        c, s = (
            [jnp.concatenate([part] * PARTS, axis=1) for part in split_parts(coef[i, f], side, 1)[2:]]
            for i in range(2)
        )
        for k, value in enumerate(stencil(c[0], s[0], c[1], s[1])):
            beta[1, k, f] = value

    loop(faces, coefficients_y)
    for start in (PAD - 8, PAD + side):
        prod[:, :, start : start + 8, :] = jnp.zeros((slots, 7, 8, lanes), jnp.float32)
    part_id = lax.broadcasted_iota(jnp.int32, (side, lanes), 1) >> (side.bit_length() - 1)
    edge_id = lax.broadcasted_iota(jnp.int32, (8, lanes), 0)
    mirror_id = lax.broadcasted_iota(jnp.int32, (8, 128), 1)
    mirror_id = mirror_id ^ (side - 1)
    upside_id = 7 - lax.broadcasted_iota(jnp.int32, (8, 128), 0)

    def by_lanes(fun, value):
        return jnp.concatenate([fun(value[:, at : at + 128]) for at in range(0, lanes, 128)], axis=1)

    def mirrored(value):
        return by_lanes(lambda chunk: jnp.take_along_axis(chunk, mirror_id, axis=1), value)

    def upside(value):
        return by_lanes(lambda chunk: jnp.take_along_axis(chunk, upside_id, axis=0), value)

    def sweep(d, between=None):
        def overflow(f):
            for low in range(2):
                edge_rows = slice(0, 8) if low else slice(side - 8, side)
                cells = field[f, edge_rows, :]
                rows = None
                for shift in (1, 2, 3):
                    value = beta[d, 3 - shift if low else 3 + shift, f, edge_rows, :] * cells
                    value = pltpu.roll(value, 8 - shift if low else shift, 0)
                    value = jnp.where(edge_id >= 8 - shift if low else edge_id < shift, value, 0.0)
                    rows = value if rows is None else rows + value
                orders = (rows, upside(rows))
                for order in range(2):
                    value = orders[order ^ low]
                    rim[0, order, f, low] = value
                    rim[1, order, f, low] = mirrored(value)

        def apply(f):
            cells = field[f]
            here = prod.at[f % slots]
            middle = beta[d, 3, f] * cells
            for k in range(7):
                if k != 3:
                    here[k, PAD : PAD + side, :] = beta[d, k, f] * cells
            for k in (0, 1, 2, 4, 5, 6):
                middle = middle + here[k, PAD + 3 - k : PAD + 3 - k + side, :]
            acc[f] = middle

        loop(faces, overflow)
        loop(faces, apply)
        if between:
            between()

        def seam(f, edge):
            code = partner_ref[f, edge]
            value = rim[flip_ref[f, edge], int(edge < 2), code >> 2, (code & 3) >> 1]
            return jnp.where((code & 1) == d, value, 0.0)

        def with_seams(value, f, axis):
            return jnp.concatenate(
                [
                    value[0:8] + seam(f, axis + 2),
                    value[8 : side - 8],
                    value[side - 8 :] + seam(f, axis),
                ],
                axis=0,
            )

        def merge(f):
            block = joined(turned_parts(with_seams(acc[f], f, d), side), part_id)
            field[f] = with_seams(block, f, 1 - d)

        loop(faces, merge)

    def between():
        loop(faces, coefficients_x)
        for copy in copies:
            copy.wait()

    for step in range(STEPS):
        sweep(1, None if step else between)
        sweep(0)

    half = 8 // group
    row_id = lax.broadcasted_iota(jnp.int32, (8, slot_lanes), 0) >> (half.bit_length() - 1)
    place = place_id

    def tiles_to_rows(block):
        value = block
        for delta in range(1 - group, group):
            if delta:
                piece = pltpu.roll(block, -half * delta % 8, 0)
                piece = pltpu.roll(piece, delta * cx % slot_lanes, 1)
                value = jnp.where(place - row_id == delta, piece, value)
        return value

    count = cy // group

    def hand_out(i):
        f, rows = row_block(i)
        strip = field[f, rows, :]
        for part in range(0, cy, 8):
            block = strip[part : part + 8]
            for first in range(0, tiles_wide, group):
                if group == tiles_wide:
                    value = block
                else:
                    value = jnp.concatenate(
                        [piece[:, first * cx : first * cx + span] for piece in split_parts(block, side, 1)],
                        axis=1,
                    )
                value = tiles_to_rows(value)
                base = (i * tiles_wide + first) * count
                if cy == 8:
                    out_ref[pl.ds(base if isinstance(i, int) else pl.multiple_of(base, 8), 8), :] = value
                else:
                    for a in range(group):
                        out_ref[pl.ds(base + a * count + part // 8 * half, half), :] = value[a * half : (a + 1) * half]

    loop(faces * tiles_high, hand_out)


def in_hbm(array):
    return pltpu.with_memory_space_constraint(array, pltpu.HBM)


def grant(*shapes):
    size = 0
    for *major, rows, columns in shapes:
        size += 4 * math.prod(major) * (-(-rows // 8) * 8) * (-(-columns // 128) * 128)
    return pltpu.CompilerParams(vmem_limit_bytes=size + size // 4 + (2 << 20))


def on_device(cotangent, courant_x, edge_x, courant_y, edge_y, cell_area, seam_partner, seam_flip):
    cells = cotangent[0]
    cy, cx, lanes = cells.shape
    levels = courant_x.shape[-1]
    faces, tiles_high, tiles_wide = (lax.axis_size(axis) for axis in ("face", "ty", "tx"))
    devices = faces * tiles_high * tiles_wide
    side = cx * tiles_wide
    width = PARTS * side
    group = 128 // (PARTS * cx)
    if lanes != PARTS * levels or devices % levels or side != cy * tiles_high:
        raise ValueError("unsupported sizes")
    if cx != 8 or cy % 8 or tiles_wide % group or 128 % side:
        raise ValueError("unsupported tile")
    f32 = jnp.float32
    slot = PARTS * group * cx

    arguments = (
        cells,
        jnp.swapaxes(courant_x[0], 0, 1),
        edge_x[0],
        courant_y[0],
        jnp.swapaxes(edge_y[0], 0, 1),
        cell_area[0],
        seam_partner,
        seam_flip,
    )
    count_in = cy * 3 // 4
    pack_rows = (count_in * group * cx, lanes)
    send, partner, flip = pl.pallas_call(
        pack_kernel,
        out_shape=(
            jax.ShapeDtypeStruct((levels * count_in, slot), f32),
            jax.ShapeDtypeStruct(seam_partner.shape, jnp.int32),
            jax.ShapeDtypeStruct(seam_flip.shape, jnp.int32),
        ),
        in_specs=[HBM] * 8,
        out_specs=(VMEM, VMEM, VMEM),
        scratch_shapes=[
            pltpu.VMEM(pack_rows, f32),
            *[pltpu.VMEM(argument.shape, f32) for argument in arguments[:6]],
            pltpu.SemaphoreType.DMA((8,)),
        ],
        compiler_params=grant(*[cells.shape] * 4, pack_rows, (levels, cy, slot)),
        name="pack",
    )(*map(in_hbm, arguments))
    if devices > levels:
        send = jnp.tile(send, (devices // levels, 1))
    pairs = send.reshape(devices * count_in // 2, 2, slot)
    spheres = lax.all_to_all(pairs, AXES, 0, 0, tiled=True).reshape(devices * count_in, slot)
    scratch = [
        (2, 7, faces, side, width),
        (2, faces, side, width),
        (faces, side, width),
        (faces, side, width),
        (min(faces, 2), 7, side + 2 * PAD, width),
        (2, 2, faces, 2, 8, width),
    ]
    back = (devices * cy // group, slot)
    result = pl.pallas_call(
        functools.partial(sphere_kernel, tiles_high, tiles_wide),
        out_shape=jax.ShapeDtypeStruct(back, f32),
        in_specs=[VMEM, VMEM, VMEM],
        out_specs=VMEM,
        scratch_shapes=[
            *[pltpu.VMEM(shape, f32) for shape in scratch],
            pltpu.SMEM(seam_partner.shape, jnp.int32),
            pltpu.SMEM(seam_flip.shape, jnp.int32),
            pltpu.SemaphoreType.DMA((2,)),
        ],
        compiler_params=grant(spheres.shape, back, *scratch),
        name="sphere",
    )(partner, flip, spheres)
    strips = lax.all_to_all(result, AXES, 0, 0, tiled=True)[: levels * cy // group]
    return pl.pallas_call(
        unpack_kernel,
        out_shape=jax.ShapeDtypeStruct(cells.shape, f32),
        in_specs=[VMEM],
        out_specs=VMEM,
        compiler_params=grant(cells.shape, strips.shape),
        name="unpack",
    )(strips)[None]


def solution(mesh):
    placed = (
        P("face", "ty", "tx", None),
        P("face", "ty", "tx", None),
        P("face", "ty", "tx"),
        P("face", "ty", "tx", None),
        P("face", "ty", "tx"),
        P("face", "ty", "tx"),
        P(),
        P(),
    )
    return jax.shard_map(
        on_device,
        mesh=mesh,
        in_specs=placed,
        out_specs=P("face", "ty", "tx", None),
        check_vma=False,
    )
```

```python
import functools
import math

import jax
import jax.numpy as jnp
from jax import lax
from jax.experimental import pallas as pl
from jax.experimental.pallas import tpu as pltpu
from jax.sharding import PartitionSpec as P

STEPS = 2
AXES = ("ty", "face", "tx")
PARTS = 4
PAD = 16
VMEM = pl.BlockSpec(memory_space=pltpu.VMEM)
HBM = pl.BlockSpec(memory_space=pltpu.HBM)


def loop(count, body):
    if count <= 8:
        for i in range(count):
            body(i)
    else:
        lax.fori_loop(0, count, lambda i, carry: (body(i), carry)[1], 0)


def split_parts(block, width, axis):
    return [lax.slice_in_dim(block, q * width, (q + 1) * width, axis=axis) for q in range(PARTS)]


def turned_parts(block, rows):
    if block.shape[0] * PARTS == 128:
        return split_parts(jnp.concatenate([block] * PARTS, axis=0).T, rows, 0)
    return [jnp.concatenate([part] * PARTS, axis=1) for part in split_parts(block.T, rows, 0)]


def joined(parts, part_id):
    value = parts[0]
    for q in range(1, PARTS):
        value = jnp.where(part_id == q, parts[q], value)
    return value


def pack_kernel(
    cot_hbm,
    cx_hbm,
    ex_hbm,
    cy_hbm,
    ey_hbm,
    area_hbm,
    partner_hbm,
    flip_hbm,
    send_ref,
    partner_ref,
    flip_ref,
    rows_ref,
    cot_ref,
    cx_ref,
    ex_ref,
    cy_ref,
    ey_ref,
    area_ref,
    sems,
):
    cy, cx = area_ref.shape
    lanes = rows_ref.shape[1]
    levels = lanes // PARTS
    group = 128 // (PARTS * cx)
    span = group * cx
    count = cy * 3 // 4
    place = [pl.multiple_of(((lax.axis_index("tx") + j) & (group - 1)) * cx, cx) for j in range(4)]

    def home(y, j):
        part, row = y // 8 * 6, y % 8
        if row < 6:
            return (part + row) * span + place[j]
        return (part + (row - 6) * 3 + j) * span + place[3]

    copies = [
        pltpu.make_async_copy(source, target, sems.at[i])
        for i, (source, target) in enumerate(
            [(cx_hbm, cx_ref), (cy_hbm, cy_ref), (cot_hbm, cot_ref), (ex_hbm, ex_ref), (ey_hbm, ey_ref)]
            + [(area_hbm, area_ref)]
            + [(partner_hbm, partner_ref), (flip_hbm, flip_ref)]
        )
    ]
    for copy in copies:
        copy.start()
    for copy in copies[:-2]:
        copy.wait()
    for y in range(cy):
        rows_ref[pl.ds(home(y, 0), cx), :] = cot_ref[y]
    along_x = [jnp.concatenate([cx_ref[x], cx_ref[x + 1]], axis=1) for x in range(cx)]
    along_y = [jnp.concatenate([cy_ref[y], cy_ref[y + 1]], axis=1) for y in range(cy)]
    for x, value in enumerate(along_x):
        for y in range(0, cy, 8):
            rows_ref[pl.ds(home(y, 1) + x, 6, stride=span), 0 : 2 * levels] = value[y : y + 6]
            rows_ref[pl.ds(home(y + 6, 1) + x, 2, stride=3 * span), 0 : 2 * levels] = value[y + 6 : y + 8]
    for y, value in enumerate(along_y):
        rows_ref[pl.ds(home(y, 1), cx), 2 * levels :] = value

    area = 12.0 * area_ref[...]
    ey = ey_ref[...].T
    gap = jnp.zeros((cy, span - cx), jnp.float32)
    metric = []
    for length in (ex_ref[:, 0:cx], ex_ref[:, 1 : cx + 1], ey[0:cy], ey[1 : cy + 1]):
        metric += [length / area, gap]
    metric = jnp.concatenate(metric, axis=1)
    lane_id = lax.broadcasted_iota(jnp.int32, (levels, lanes), 1)
    first_lane = (lane_id & (span - 1)) & ~(cx - 1)
    metrics = [(first_lane == place[j], pltpu.roll(metric, place[j], 1)) for j in (2, 3)]

    part_id = lane_id >> (span.bit_length() - 1)
    for r in range(count):
        row = joined(turned_parts(rows_ref[r * span : (r + 1) * span], levels), part_id)
        y = r // 6 * 8 + r % 6
        row = jnp.where(metrics[0][0], metrics[0][1][y : y + 1], row)
        if r % 3 == 2:
            y = r // 6 * 8 + 6 + r % 6 // 3
            row = jnp.where(metrics[1][0], metrics[1][1][y : y + 1], row)
        send_ref[pl.ds(r, levels, stride=count), :] = row
    for copy in copies[-2:]:
        copy.wait()


def unpack_kernel(recv_ref, out_ref):
    cy, cx, lanes = out_ref.shape
    levels = lanes // PARTS
    group = 128 // (PARTS * cx)
    half = 8 // group
    count = cy // group
    part_id = lax.broadcasted_iota(jnp.int32, (cx, lanes), 1) >> (levels.bit_length() - 1)
    for r in range(count):
        pieces = turned_parts(recv_ref[pl.ds(r, levels, stride=count), :], group * cx)
        for b in range(group):
            out_ref[r // half * 8 + b * half + r % half] = joined(
                [piece[b * cx : (b + 1) * cx] for piece in pieces], part_id
            )


def stencil(*parts):
    c_low, f_low, c_high, f_high = parts

    def interface(c, f):
        size = jnp.abs(c)
        rest = 1.0 - size
        part = f * size
        centre = f * rest * rest
        outer = part * rest
        cell = part * (12.0 + 24.0 * rest)
        middle = 7.0 * centre
        cell = cell - 7.0 * outer
        plus = c > 0
        first = jnp.where(plus, outer, 0.0)
        last = outer - first
        return (
            first,
            -7.0 * first - centre,
            middle + jnp.where(plus, cell, outer),
            middle + jnp.where(plus, outer, cell),
            -7.0 * last - centre,
            last,
        )

    low, high = interface(c_low, f_low), interface(c_high, f_high)
    return (
        low[0],
        low[1] - high[0],
        low[2] - high[1],
        1.0 + low[3] - high[2],
        low[4] - high[3],
        low[5] - high[4],
        -high[5],
    )


def sphere_kernel(
    tiles_high,
    tiles_wide,
    partner_vmem,
    flip_vmem,
    recv_ref,
    out_ref,
    beta,
    coef,
    acc,
    field,
    prod,
    rim,
    partner_ref,
    flip_ref,
    sems,
):
    copies = [
        pltpu.make_async_copy(partner_vmem, partner_ref, sems.at[0]),
        pltpu.make_async_copy(flip_vmem, flip_ref, sems.at[1]),
    ]
    for copy in copies:
        copy.start()
    faces, side, lanes = field.shape
    cy, cx = side // tiles_high, side // tiles_wide
    slots = prod.shape[0]
    slot_lanes = recv_ref.shape[1]
    group = slot_lanes // (PARTS * cx)
    span = group * cx
    lane_id = lax.broadcasted_iota(jnp.int32, (8, slot_lanes), 1)
    place_id = (lane_id >> (cx.bit_length() - 1)) & (group - 1)

    def row_block(i):
        f, ty = i % faces, i // faces
        start = ty * cy
        return f, pl.ds(start if isinstance(i, int) else pl.multiple_of(start, 8), cy)

    count_in = cy * 3 // 4

    def spread(tiles):
        blocks = []
        for j in range(4):
            block = tiles[0]
            for tx in range(1, group):
                block = jnp.where(place_id[0:6] == (tx + j) % group, tiles[tx], block)
            if j:
                ahead = pltpu.roll(block, slot_lanes - j * cx, 1)
                around = pltpu.roll(block, span - j * cx, 1)
                block = jnp.where(place_id[0:6] < group - j, ahead, around)
            blocks.append(block)
        last = blocks[3]
        return [
            jnp.concatenate([blocks[j], last[j : j + 1], last[3 + j : 4 + j]], axis=0) for j in range(3)
        ]

    def assemble(i):
        f, rows = row_block(i)
        for part in range(cy // 8):
            groups = []
            for first in range(0, tiles_wide, group):
                start = (i * tiles_wide + first) * count_in + part * 6
                groups.append(spread([recv_ref[pl.ds(start + tx * count_in, 6), :] for tx in range(group)]))
            values = []
            for blocks in zip(*groups):
                if len(blocks) == 1:
                    values.append(blocks[0])
                    continue
                values.append(
                    jnp.concatenate(
                        [block[:, q * span : (q + 1) * span] for q in range(PARTS) for block in blocks],
                        axis=1,
                    )
                )
            cells, courant, metric = values
            here = pl.ds(i // faces * cy + part * 8, 8)
            if not isinstance(i, int):
                here = pl.ds(pl.multiple_of(i // faces * cy + part * 8, 8), 8)
            field[f, here, :] = cells
            coef[0, f, here, :] = courant
            coef[1, f, here, :] = courant * metric

    loop(faces * tiles_high, assemble)

    def coefficients_x(f):
        c, s = turned_parts(coef[0, f], side), turned_parts(coef[1, f], side)
        for k, value in enumerate(stencil(c[0], s[0], c[1], s[1])):
            beta[0, k, f] = value

    def coefficients_y(f):
        c, s = (
            [jnp.concatenate([part] * PARTS, axis=1) for part in split_parts(coef[i, f], side, 1)[2:]]
            for i in range(2)
        )
        for k, value in enumerate(stencil(c[0], s[0], c[1], s[1])):
            beta[1, k, f] = value

    loop(faces, coefficients_y)
    for start in (PAD - 8, PAD + side):
        prod[:, :, start : start + 8, :] = jnp.zeros((slots, 7, 8, lanes), jnp.float32)
    part_id = lax.broadcasted_iota(jnp.int32, (side, lanes), 1) >> (side.bit_length() - 1)
    edge_id = lax.broadcasted_iota(jnp.int32, (8, lanes), 0)
    mirror_id = lax.broadcasted_iota(jnp.int32, (8, 128), 1)
    mirror_id = mirror_id ^ (side - 1)
    upside_id = 7 - lax.broadcasted_iota(jnp.int32, (8, 128), 0)

    def by_lanes(fun, value):
        return jnp.concatenate([fun(value[:, at : at + 128]) for at in range(0, lanes, 128)], axis=1)

    def mirrored(value):
        return by_lanes(lambda chunk: jnp.take_along_axis(chunk, mirror_id, axis=1), value)

    def upside(value):
        return by_lanes(lambda chunk: jnp.take_along_axis(chunk, upside_id, axis=0), value)

    def sweep(d, between=None):
        def overflow(f):
            for low in range(2):
                edge_rows = slice(0, 8) if low else slice(side - 8, side)
                cells = field[f, edge_rows, :]
                rows = None
                for shift in (1, 2, 3):
                    value = beta[d, 3 - shift if low else 3 + shift, f, edge_rows, :] * cells
                    value = pltpu.roll(value, 8 - shift if low else shift, 0)
                    value = jnp.where(edge_id >= 8 - shift if low else edge_id < shift, value, 0.0)
                    rows = value if rows is None else rows + value
                orders = (rows, upside(rows))
                for order in range(2):
                    value = orders[order ^ low]
                    rim[0, order, f, low] = value
                    rim[1, order, f, low] = mirrored(value)

        def apply(f):
            cells = field[f]
            here = prod.at[f % slots]
            middle = beta[d, 3, f] * cells
            for k in range(7):
                if k != 3:
                    here[k, PAD : PAD + side, :] = beta[d, k, f] * cells
            for k in (0, 1, 2, 4, 5, 6):
                middle = middle + here[k, PAD + 3 - k : PAD + 3 - k + side, :]
            acc[f] = middle

        loop(faces, overflow)
        loop(faces, apply)
        if between:
            between()

        def seam(f, edge):
            code = partner_ref[f, edge]
            value = rim[flip_ref[f, edge], int(edge < 2), code >> 2, (code & 3) >> 1]
            return jnp.where((code & 1) == d, value, 0.0)

        def with_seams(value, f, axis):
            return jnp.concatenate(
                [
                    value[0:8] + seam(f, axis + 2),
                    value[8 : side - 8],
                    value[side - 8 :] + seam(f, axis),
                ],
                axis=0,
            )

        if lanes == 128:
            blocks = [turned_parts(with_seams(acc[f], f, d), side) for f in range(faces)]
            for f in range(faces):
                field[f] = with_seams(joined(blocks[f], part_id), f, 1 - d)
        else:

            def merge(f):
                block = joined(turned_parts(with_seams(acc[f], f, d), side), part_id)
                field[f] = with_seams(block, f, 1 - d)

            loop(faces, merge)

    def between():
        loop(faces, coefficients_x)
        for copy in copies:
            copy.wait()

    for step in range(STEPS):
        sweep(1, None if step else between)
        sweep(0)

    half = 8 // group
    row_id = lax.broadcasted_iota(jnp.int32, (8, slot_lanes), 0) >> (half.bit_length() - 1)
    place = place_id

    def tiles_to_rows(block):
        value = block
        for delta in range(1 - group, group):
            if delta:
                piece = pltpu.roll(block, -half * delta % 8, 0)
                piece = pltpu.roll(piece, delta * cx % slot_lanes, 1)
                value = jnp.where(place - row_id == delta, piece, value)
        return value

    count = cy // group

    def hand_out(i):
        f, rows = row_block(i)
        strip = field[f, rows, :]
        for part in range(0, cy, 8):
            block = strip[part : part + 8]
            for first in range(0, tiles_wide, group):
                if group == tiles_wide:
                    value = block
                else:
                    value = jnp.concatenate(
                        [piece[:, first * cx : first * cx + span] for piece in split_parts(block, side, 1)],
                        axis=1,
                    )
                value = tiles_to_rows(value)
                base = (i * tiles_wide + first) * count
                if cy == 8:
                    out_ref[pl.ds(base if isinstance(i, int) else pl.multiple_of(base, 8), 8), :] = value
                else:
                    for a in range(group):
                        out_ref[pl.ds(base + a * count + part // 8 * half, half), :] = value[a * half : (a + 1) * half]

    loop(faces * tiles_high, hand_out)


def in_hbm(array):
    return pltpu.with_memory_space_constraint(array, pltpu.HBM)


def grant(*shapes):
    size = 0
    for *major, rows, columns in shapes:
        size += 4 * math.prod(major) * (-(-rows // 8) * 8) * (-(-columns // 128) * 128)
    return pltpu.CompilerParams(vmem_limit_bytes=size + size // 4 + (2 << 20))


def on_device(cotangent, courant_x, edge_x, courant_y, edge_y, cell_area, seam_partner, seam_flip):
    cells = cotangent[0]
    cy, cx, lanes = cells.shape
    levels = courant_x.shape[-1]
    faces, tiles_high, tiles_wide = (lax.axis_size(axis) for axis in ("face", "ty", "tx"))
    devices = faces * tiles_high * tiles_wide
    side = cx * tiles_wide
    width = PARTS * side
    group = 128 // (PARTS * cx)
    if lanes != PARTS * levels or devices % levels or side != cy * tiles_high:
        raise ValueError("unsupported sizes")
    if cx != 8 or cy % 8 or tiles_wide % group or 128 % side:
        raise ValueError("unsupported tile")
    f32 = jnp.float32
    slot = PARTS * group * cx

    arguments = (
        cells,
        jnp.swapaxes(courant_x[0], 0, 1),
        edge_x[0],
        courant_y[0],
        jnp.swapaxes(edge_y[0], 0, 1),
        cell_area[0],
        seam_partner,
        seam_flip,
    )
    count_in = cy * 3 // 4
    pack_rows = (count_in * group * cx, lanes)
    send, partner, flip = pl.pallas_call(
        pack_kernel,
        out_shape=(
            jax.ShapeDtypeStruct((levels * count_in, slot), f32),
            jax.ShapeDtypeStruct(seam_partner.shape, jnp.int32),
            jax.ShapeDtypeStruct(seam_flip.shape, jnp.int32),
        ),
        in_specs=[HBM] * 8,
        out_specs=(VMEM, VMEM, VMEM),
        scratch_shapes=[
            pltpu.VMEM(pack_rows, f32),
            *[pltpu.VMEM(argument.shape, f32) for argument in arguments[:6]],
            pltpu.SemaphoreType.DMA((8,)),
        ],
        compiler_params=grant(*[cells.shape] * 4, pack_rows, (levels, cy, slot)),
        name="pack",
    )(*map(in_hbm, arguments))
    if devices > levels:
        send = jnp.tile(send, (devices // levels, 1))
    pairs = send.reshape(devices * count_in // 2, 2, slot)
    spheres = lax.all_to_all(pairs, AXES, 0, 0, tiled=True).reshape(devices * count_in, slot)
    scratch = [
        (2, 7, faces, side, width),
        (2, faces, side, width),
        (faces, side, width),
        (faces, side, width),
        (min(faces, 2), 7, side + 2 * PAD, width),
        (2, 2, faces, 2, 8, width),
    ]
    back = (devices * cy // group, slot)
    result = pl.pallas_call(
        functools.partial(sphere_kernel, tiles_high, tiles_wide),
        out_shape=jax.ShapeDtypeStruct(back, f32),
        in_specs=[VMEM, VMEM, VMEM],
        out_specs=VMEM,
        scratch_shapes=[
            *[pltpu.VMEM(shape, f32) for shape in scratch],
            pltpu.SMEM(seam_partner.shape, jnp.int32),
            pltpu.SMEM(seam_flip.shape, jnp.int32),
            pltpu.SemaphoreType.DMA((2,)),
        ],
        compiler_params=grant(spheres.shape, back, *scratch),
        name="sphere",
    )(partner, flip, spheres)
    strips = lax.all_to_all(result, AXES, 0, 0, tiled=True)[: levels * cy // group]
    return pl.pallas_call(
        unpack_kernel,
        out_shape=jax.ShapeDtypeStruct(cells.shape, f32),
        in_specs=[VMEM],
        out_specs=VMEM,
        compiler_params=grant(cells.shape, strips.shape),
        name="unpack",
    )(strips)[None]


def solution(mesh):
    placed = (
        P("face", "ty", "tx", None),
        P("face", "ty", "tx", None),
        P("face", "ty", "tx"),
        P("face", "ty", "tx", None),
        P("face", "ty", "tx"),
        P("face", "ty", "tx"),
        P(),
        P(),
    )
    return jax.shard_map(
        on_device,
        mesh=mesh,
        in_specs=placed,
        out_specs=P("face", "ty", "tx", None),
        check_vma=False,
    )
```
